256 devices in a mesh: depth: 8 (over z), lateral: 32 (over x, y, core).
Axes of the slice: x: 4, y: 4, z: 8, core: 2. Of those that a mesh axis runs over, the one named last changes fastest.
Arguments:
- samples: bfloat16 [8, 32, 64, 8192], P('depth', 'lateral'), may hold values from -6 to 6
- w_first: bfloat16 [8, 32, 64, 256], P('depth', 'lateral'), may hold values from -0.75 to 0.75
- w_second: bfloat16 [8, 32, 256, 256], P('depth', 'lateral'), may hold values from -0.5 to 0.5
- w_third: bfloat16 [8, 32, 256, 512], P('depth', 'lateral'), may hold values from -0.5 to 0.5
- w_density: bfloat16 [8, 32, 256], P('depth', 'lateral'), may hold values from -0.5 to 0.5
- decoder: float32 [32, 3, 512], P('lateral'), may hold values from -1 to 1
- depth_order: int32 [32, 8], P('lateral'), may hold values from 0 to 7, each once within a row
- ray_slot: int32 [32, 1024], P('lateral'), may hold values from 0 to 127, as said below
- target: float32 [32, 3, 256], P('lateral', None, 'depth'), may hold values from -24 to 24
Outputs:
- grad_first: float32 [8, 32, 64, 256], P('depth', 'lateral')
- grad_second: float32 [8, 32, 256, 256], P('depth', 'lateral')
- grad_third: float32 [8, 32, 256, 512], P('depth', 'lateral')
- grad_density: float32 [8, 32, 256], P('depth', 'lateral')
- grad_decoder: float32 [32, 3, 512], P('lateral')
- mean_error: float32 [], replicated
The draws below stay inside these ranges and needn't reach their ends.
Inputs may be any that keep to these rules, and one draw needn't show every extreme that they name: `ray_slot`: in each row, every aligned block of 128 entries holds each of 0 to 127 once. `depth_order`: each row names every tile once.
All inputs are finite; a program needn't handle non-finite values.
Results may differ from the reference program's by a relative error of at most 0.017.
The reference program's roundings to bfloat16 on the way (of `features`, `scaled`, `ray_feature`, `ray_grad`, `logit_grad`, `feature_grad`, `back_two` and `back_one`) count: a program that leaves them out, or rounds other values in their place, can miss the bound.
Values may be sent and summed in bfloat16 or wider, within the bound.
A program may use at most 128 MiB of HBM per device.

```python
import jax
import jax.numpy as jnp
from jax import lax

ENC = 64
HID = 256
FEAT = 512
SAMPLES = 8
SPP = 4
RAYS = 1024
TILES = 8
COLS = 32
SHARE = 128
SLOTS = 4
PIXELS = 256
PIX_SHARE = 32


def draw_ray_slot(key, part):
    blocks = jax.random.split(key, COLS * TILES)
    orders = jax.vmap(lambda single: jax.random.permutation(single, SHARE))(blocks)
    return orders.reshape(COLS, RAYS).astype(jnp.int32)


def draw_target(key, part):
    inner = jax.random.fold_in(key, 7)
    pixel_pos = jnp.arange(PIXELS, dtype=jnp.float32) / max(PIXELS - 1, 1)
    column_pos = jnp.arange(COLS, dtype=jnp.float32) / max(COLS - 1, 1)
    rising = (0.4 + 1.6 * column_pos)[:, None, None] * (0.4 + 1.6 * pixel_pos)[None, None, :]
    noise = jnp.clip(jax.random.normal(inner, (COLS, 3, PIXELS), jnp.float32), -6.0, 6.0)
    return (noise * rising).astype(jnp.float32)


def block_levels(rng, shape, shards, smallest, largest):
    def one(position, blocks):
        heights = jax.random.uniform(jax.random.fold_in(jax.random.fold_in(rng, 6), position), (blocks,), jnp.float32, smallest / len(shards), largest / len(shards))
        return jnp.repeat(jnp.exp(heights), shape[position] // blocks).reshape((-1,) + (1,) * (len(shape) - position - 1))

    gain = one(*shards[0])
    for cut in shards[1:]:
        gain = gain * one(*cut)
    return gain


def normal_values(rng, dims, spread, reach, cuts=(), kind=jnp.bfloat16):
    drawn = jax.random.normal(rng, dims, jnp.float32) * spread
    if len(cuts) > 0:
        drawn = block_levels(rng, dims, cuts, -0.22, 0.18) * drawn
    return jnp.clip(drawn, min=-reach, max=reach).astype(kind)


def setup_inputs(seed: int = 0) -> dict:
    arg_keys = jax.random.split(jax.random.key(seed), 10)
    samples = normal_values(arg_keys[0], (TILES, COLS, ENC, SAMPLES * RAYS), 1.0, 6.0, ((0, 8), (1, 32)))
    w_first = normal_values(arg_keys[1], (TILES, COLS, ENC, HID), ENC ** -0.5, 0.75, ((0, 8), (1, 32)))
    w_second = normal_values(arg_keys[2], (TILES, COLS, HID, HID), (HID // 2) ** -0.5, 0.5, ((0, 8), (1, 32)))
    w_third = normal_values(arg_keys[3], (TILES, COLS, HID, FEAT), (HID // 2) ** -0.5, 0.5, ((0, 8), (1, 32)))
    w_density = normal_values(arg_keys[4], (TILES, COLS, HID), (HID // 2) ** -0.5, 0.5, ((0, 8), (1, 32)))
    decoder = normal_values(arg_keys[5], (COLS, 3, FEAT), (FEAT // 16) ** -0.5, 1.0, ((0, 32),), jnp.float32)
    depth_order = jax.vmap(lambda own: jax.random.permutation(own, TILES))(jax.random.split(arg_keys[6], COLS)).reshape((COLS, TILES)).astype(jnp.int32)
    ray_slot = draw_ray_slot(jax.random.fold_in(arg_keys[9], 71), 0)
    target = draw_target(jax.random.fold_in(arg_keys[9], 71), 0)
    return {"samples": samples, "w_first": w_first, "w_second": w_second, "w_third": w_third, "w_density": w_density, "decoder": decoder, "depth_order": depth_order, "ray_slot": ray_slot, "target": target}


step_length = 0.04
norm_floor = 1e-05
exact_mode = lax.Precision.HIGHEST

def network(inputs, w_first, w_second, w_third, w_density):
    contract_lead = (((0,), (0,)), ((), ()))
    hidden_one = jnp.maximum(lax.dot_general(w_first, inputs, contract_lead, preferred_element_type=jnp.float32), 0.0).astype(jnp.bfloat16)
    hidden_two = jnp.maximum(lax.dot_general(w_second, hidden_one, contract_lead, preferred_element_type=jnp.float32), 0.0).astype(jnp.bfloat16)
    features = lax.dot_general(w_third, hidden_two, contract_lead, preferred_element_type=jnp.float32).astype(jnp.bfloat16)
    logits = jnp.dot(w_density, hidden_two, preferred_element_type=jnp.float32)
    return (hidden_one, hidden_two, features, logits)

def segment(density):
    before_here = step_length * (jnp.cumsum(density, axis=0) - density)
    weights = jnp.exp(-before_here) * (1.0 - jnp.exp(-step_length * density))
    return (weights, step_length * lax.optimization_barrier(jnp.sum(density, axis=0)))

def blend_samples(features, weights):
    sample_count = weights.shape[0]
    blocks = features.reshape(features.shape[0], sample_count, weights.shape[1])
    total = jnp.zeros((features.shape[0], weights.shape[1]), jnp.float32)
    for sample in range(sample_count):
        total = total + blocks[:, sample].astype(jnp.float32) * weights[sample][None]
    return total

def tile_forward(inputs, w_first, w_second, w_third, w_density, sample_count):
    hidden_one, hidden_two, features, logits = network(inputs, w_first, w_second, w_third, w_density)
    density = jax.nn.softplus(logits).reshape(sample_count, -1)
    weights, depth_sum = segment(density)
    return (hidden_one, hidden_two, features, logits, weights, depth_sum)

def tile_backward(inputs, w_first, w_second, w_third, w_density, hidden_one, hidden_two, features, logits, feat_grad, depth_grad, sample_count):
    density = jax.nn.softplus(logits).reshape(sample_count, -1)
    outputs, pullback = jax.vjp(segment, density)
    weights = outputs[0]
    blocks = features.reshape(features.shape[0], sample_count, -1)
    weight_grad = jnp.stack([lax.optimization_barrier(jnp.sum(blocks[:, sample].astype(jnp.float32) * feat_grad, axis=0)) for sample in range(sample_count)])
    density_grad = pullback((weight_grad, depth_grad))[0]
    logit_grad = (density_grad * jax.nn.sigmoid(logits.reshape(sample_count, -1))).reshape(-1).astype(jnp.bfloat16)
    feature_grad = (weights[None] * feat_grad[:, None]).astype(jnp.bfloat16).reshape(features.shape)
    contract_rows = (((1,), (1,)), ((), ()))
    grad_third = lax.dot_general(hidden_two, feature_grad, contract_rows, preferred_element_type=jnp.float32)
    grad_density = jnp.dot(hidden_two, logit_grad, preferred_element_type=jnp.float32)
    back_two = jnp.dot(w_third, feature_grad, preferred_element_type=jnp.float32)
    back_two = back_two + w_density.astype(jnp.float32)[:, None] * logit_grad.astype(jnp.float32)[None]
    back_two = jnp.where(hidden_two > 0, back_two, 0.0).astype(jnp.bfloat16)
    grad_second = lax.dot_general(hidden_one, back_two, contract_rows, preferred_element_type=jnp.float32)
    back_one = jnp.where(hidden_one > 0, jnp.dot(w_second, back_two, preferred_element_type=jnp.float32), 0.0).astype(jnp.bfloat16)
    grad_first = lax.dot_general(inputs, back_one, contract_rows, preferred_element_type=jnp.float32)
    return (grad_first, grad_second, grad_third, grad_density)

def reference(samples, w_first, w_second, w_third, w_density, decoder, depth_order, ray_slot, target):

    def forward_column(column):

        def forward_tile(tile):
            outputs = tile_forward(samples[tile, column], w_first[tile, column], w_second[tile, column], w_third[tile, column], w_density[tile, column], SAMPLES)
            return (blend_samples(outputs[2], outputs[4]), outputs[5])
        return lax.map(forward_tile, jnp.arange(TILES, dtype=jnp.int32))
    blended, depth_sums = lax.map(forward_column, jnp.arange(COLS, dtype=jnp.int32))
    ranks = jnp.arange(TILES, dtype=jnp.int32)
    places = lax.optimization_barrier(jnp.sum(ranks[None, :, None] * (depth_order[:, :, None] == ranks[None, None, :]).astype(jnp.int32), axis=1))
    earlier = (places[:, None, :] < places[:, :, None]).astype(jnp.float32)
    before = jnp.einsum('ckj,cjr->ckr', earlier, depth_sums, precision=exact_mode)
    scale = jnp.exp(-before)
    scaled = (scale[:, :, None, :] * blended).astype(jnp.bfloat16)
    ray_feature = lax.optimization_barrier(jnp.sum(scaled.astype(jnp.float32), axis=1)).astype(jnp.bfloat16)
    ray_index = jnp.arange(RAYS, dtype=jnp.int32)
    columns = jnp.arange(COLS, dtype=jnp.int32)[:, None]
    owner = ray_slot // SLOTS
    inside = ray_slot % SLOTS
    pixel_id = owner * PIXELS + (ray_index // SHARE)[None] * PIX_SHARE + (inside * COLS + columns) // SPP
    rows = jnp.swapaxes(ray_feature.astype(jnp.float32), 1, 2).reshape(COLS * RAYS, FEAT)
    pixel_rows = jax.ops.segment_sum(rows, pixel_id.reshape(-1), num_segments=COLS * PIXELS) / SPP
    pixel_mean = jnp.swapaxes(pixel_rows.reshape(COLS, PIXELS, FEAT), 1, 2)
    inverse = lax.rsqrt(lax.optimization_barrier(jnp.mean(pixel_mean * pixel_mean, axis=1, keepdims=True)) + norm_floor)
    normed = pixel_mean * inverse
    colors = jnp.einsum('cif,cfp->cip', decoder, normed, precision=exact_mode)
    residue = colors - target
    mean_error = jnp.sum(residue * residue) / (3 * COLS * PIXELS)
    grad_decoder = jnp.einsum('cip,cfp->cif', residue, normed, precision=exact_mode)
    normed_grad = jnp.einsum('cif,cip->cfp', decoder, residue, precision=exact_mode)
    pixel_grad = inverse * (normed_grad - normed * lax.optimization_barrier(jnp.mean(normed_grad * normed, axis=1, keepdims=True))) / SPP
    pixel_grad = jnp.swapaxes(pixel_grad, 1, 2)
    ray_grad = jnp.swapaxes(pixel_grad.reshape(COLS * PIXELS, FEAT)[pixel_id], 1, 2).astype(jnp.bfloat16)
    terms = jnp.einsum('ckfr,cfr->ckr', scaled.astype(jnp.float32), ray_grad.astype(jnp.float32))
    depth_grads = -jnp.einsum('cmk,cmr->ckr', earlier, terms, precision=exact_mode)

    def backward_column(column):

        def backward_tile(tile):
            inputs = samples[tile, column]
            weights_a = w_first[tile, column]
            weights_b = w_second[tile, column]
            weights_c = w_third[tile, column]
            weights_d = w_density[tile, column]
            outputs = tile_forward(inputs, weights_a, weights_b, weights_c, weights_d, SAMPLES)
            feat_grad = scale[column, tile][None] * ray_grad[column].astype(jnp.float32)
            return tile_backward(inputs, weights_a, weights_b, weights_c, weights_d, outputs[0], outputs[1], outputs[2], outputs[3], feat_grad, depth_grads[column, tile], SAMPLES)
        return lax.map(backward_tile, jnp.arange(TILES, dtype=jnp.int32))
    grad_first, grad_second, grad_third, grad_density = lax.map(backward_column, jnp.arange(COLS, dtype=jnp.int32))
    return (jnp.swapaxes(grad_first, 0, 1), jnp.swapaxes(grad_second, 0, 1), jnp.swapaxes(grad_third, 0, 1), jnp.swapaxes(grad_density, 0, 1), grad_decoder, mean_error)
```

```python
import jax
import jax.numpy as jnp
from jax import lax
from jax.experimental import pallas as pl
from jax.experimental.pallas import tpu as pltpu
from jax.sharding import PartitionSpec as P

MESH = pl.DeviceIdType.MESH
F32 = jnp.float32
BF16 = jnp.bfloat16

ENC, HID, FEAT = 64, 256, 512
S = 8
K = 8
R = 128
CHIPS = 16
W = S * R
HALF = FEAT // 2
STEP = 0.04
FLOOR = 1e-05
COUNT = 24576.0
LAG = 3

NN = (((1,), (0,)), ((), ()))
NT = (((1,), (1,)), ((), ()))
TN = (((0,), (0,)), ((), ()))


def mm(a, b, dims):
    return lax.dot_general(a, b, dims, preferred_element_type=F32)


def offset_of(i):
    return 4 + ((i + 1) // 2) * (1 - 2 * (i % 2))


def near_offset_of(i):
    return ((i + 1) // 2) * (2 * (i % 2) - 1) + 8


def kernel(
    x_ref, w1_ref, w2_ref, w3_ref, wd_ref, dec_ref, order_ref, slot_ref, tgt_ref,
    g1_ref, g2_ref, g3_ref, gd_ref, gdec_ref, err_ref,
    w1t, w2t, w3t, wdb, h1s, h2s, feats, lgs, wts, expi, bld, scl, scaled, oh,
    pfull, prec, zsend, zrecv, lt, lr, lb, br, gbuf, dsall, tmall, wgs, lgrad, b2s,
    decall, esend, elat, epsend, eprec,
    s_ds, r_ds, s_pf, r_pf, s_z, r_z, s_l, r_l, s_b, r_b, s_g, r_g, s_pb, r_pb,
    s_t, r_t, s_d, r_d, s_e, r_e, s_ep, r_ep,
):
    me = lax.axis_index("depth")
    lat = lax.axis_index("lateral")
    h = lat % 2
    m = lat // 2
    sib = lat + 1 - 2 * h

    def depth_peer(off):
        return (me + off) % K

    def rc(src, dst, ssem, rsem, z, l):
        return pltpu.make_async_remote_copy(
            src_ref=src, dst_ref=dst, send_sem=ssem, recv_sem=rsem,
            device_id=(z, l), device_id_type=MESH,
        )

    barrier = pltpu.get_barrier_semaphore()

    def greet_depth(e, c):
        pl.semaphore_signal(barrier, inc=1, device_id=((me + e) % K, lat), device_id_type=MESH)
        return c

    def greet_lateral(e, c):
        pl.semaphore_signal(
            barrier, inc=1, device_id=(me, ((m + e) % CHIPS) * 2 + h), device_id_type=MESH
        )
        return c

    lax.fori_loop(1, K, greet_depth, 0)
    lax.fori_loop(1, CHIPS, greet_lateral, 0)
    pl.semaphore_signal(barrier, inc=1, device_id=(me, sib), device_id_type=MESH)

    w1t[...] = w1_ref[...].T
    w2t[...] = w2_ref[...].T
    w3t[...] = w3_ref[...].T
    wd8 = jnp.broadcast_to(wd_ref[...], (8, HID))
    wdb[...] = jnp.broadcast_to(wd_ref[...].astype(F32), (R, HID)).T

    def take_x(d):
        return jnp.concatenate(
            [x_ref[:, pl.ds(pl.multiple_of(s * (K * R) + d * R, R), R)] for s in range(S)], axis=1
        )

    def first_pass(d, c):
        x = take_x(d)
        h1s[d] = jnp.maximum(mm(w1t[...], x, NN), 0.0).astype(BF16)
        h2s[d] = jnp.maximum(mm(w2t[...], h1s[d], NN), 0.0).astype(BF16)
        lg = mm(wd8, h2s[d], NN)
        lgs[d] = jnp.concatenate(
            [lg[s : s + 1, s * R : (s + 1) * R] for s in range(S)], axis=0
        )
        return c

    lax.fori_loop(0, K, first_pass, 0)

    sub = lax.broadcasted_iota(jnp.int32, (K, S, R), 1)
    logits = lgs[...]
    density = jnp.maximum(logits, 0.0) + jnp.log1p(jnp.exp(-jnp.abs(logits)))
    inc = density
    for sh in (1, 2, 4):
        inc = inc + jnp.where(sub >= sh, pltpu.roll(inc, sh, 1), 0.0)
    wts[...] = jnp.exp(-STEP * (inc - density)) * (1.0 - jnp.exp(-STEP * density))
    expi[...] = jnp.exp(-STEP * inc)
    dsall[me] = STEP * jnp.concatenate([inc[d, S - 1 : S, :] for d in range(K)], axis=0)

    pl.semaphore_wait(barrier, K - 1 + CHIPS - 1 + 1)

    def ds_copy(off, k):
        return rc(dsall.at[k], dsall.at[k], s_ds.at[off], r_ds.at[k], depth_peer(off), lat)

    def send_ds(off, c):
        ds_copy(off, me).start()
        return c

    lax.fori_loop(1, K, send_ds, 0)

    row = lax.broadcasted_iota(jnp.int32, (2 * R, R), 0)
    code = (((row // 8) % CHIPS) * 2 + row // R) * 4 + row % 4
    code_lo = jnp.where((row // 4) % 2 == 0, code, -1)
    code_hi = jnp.where((row // 4) % 2 == 1, code, -1)

    def one_hot(d, c):
        slots = slot_ref[:, pl.ds(pl.multiple_of(d * R, R), R)]
        oh[d] = jnp.concatenate(
            [
                jnp.where(code_lo == slots, 1.0, 0.0).astype(BF16),
                jnp.where(code_hi == slots, 1.0, 0.0).astype(BF16),
            ],
            axis=1,
        )
        return c

    lax.fori_loop(0, K, one_hot, 0)

    def second_pass(d, c):
        feats[d] = mm(w3t[...], h2s[d], NN).astype(BF16)
        for f0 in range(0, FEAT, 64):
            total = jnp.zeros((64, R), F32)
            for s in range(S):
                total = total + feats[d, f0 : f0 + 64, s * R : (s + 1) * R].astype(F32) * wts[
                    d, s : s + 1, :
                ]
            fh = f0 // HALF
            bld[d, f0 - fh * HALF : f0 - fh * HALF + 64, fh * R : (fh + 1) * R] = total
        return c

    lax.fori_loop(0, K, second_pass, 0)

    places = []
    mine = jnp.int32(0)
    for k in range(K):
        place = jnp.int32(0)
        for p in range(K):
            place = place + jnp.where(order_ref[0, p] == k, p, 0)
        places.append(place)
    for p in range(K):
        mine = mine + jnp.where(order_ref[0, p] == me, p, 0)

    def wait_ds(off, c):
        ds_copy(off, depth_peer(off)).wait_recv()
        return c

    lax.fori_loop(1, K, wait_ds, 0)
    before = jnp.zeros((K, R), F32)
    for k in range(K):
        before = before + dsall[k] * jnp.where(places[k] < mine, 1.0, 0.0)
    scl[...] = jnp.exp(-before)

    def pf_copy(d):
        return rc(pfull.at[d, 1 - h], prec.at[d], s_pf.at[d], r_pf.at[d], me, sib)

    def z_copy(d, k):
        return rc(zsend.at[d], zrecv.at[k], s_z.at[d], r_z.at[k], d, lat)

    def make_scaled(d):
        sc = scl[pl.ds(d, 1), :]
        sc = jnp.concatenate([sc, sc], axis=1)
        scaled[d] = (bld[d] * sc).astype(BF16)
        placed = mm(oh[d], scaled[d], NT).astype(BF16)
        pfull[d, 0] = placed[0:R]
        pfull[d, 1] = placed[R : 2 * R]
        pf_copy(d).start()

    def pair_sum(d):
        pf_copy(d).wait_recv()
        return (pfull[d, h].astype(F32) + prec[d].astype(F32)).astype(BF16)

    def send_share(i):
        d = depth_peer(offset_of(i))
        zsend[d] = pair_sum(d)
        z_copy(d, me).start()

    def scaled_step(i, c):
        make_scaled(depth_peer(offset_of(i)))

        @pl.when(i >= LAG)
        def _():
            send_share(i - LAG)

        return c

    lax.fori_loop(0, K, scaled_step, 0)
    for i in range(K - LAG, K - 1):
        send_share(i)
    zrecv[me] = pair_sum(me)

    def wait_z(off, c):
        z_copy(me, depth_peer(off)).wait_recv()
        return c

    lax.fori_loop(1, K, wait_z, 0)
    total = zrecv[0].astype(F32)
    for k in range(1, K):
        total = total + zrecv[k].astype(F32)
    lt[...] = total.reshape(CHIPS, 8, HALF)

    def l_copy(e, src):
        to = (m + e) % CHIPS
        return rc(lt.at[to], lr.at[src], s_l.at[to], r_l.at[src], me, to * 2 + h)

    def send_l(e, c):
        l_copy(e, m).start()
        return c

    lax.fori_loop(1, CHIPS, send_l, 0)
    lr[m] = lt[m]

    shape3 = (8, 8, 32)
    grp = lax.broadcasted_iota(jnp.int32, shape3, 0)
    rowq = lax.broadcasted_iota(jnp.int32, shape3, 1) % 4
    pix = lax.broadcasted_iota(jnp.int32, shape3, 2)
    chosen = pix == rowq * 8 + grp
    low = lax.broadcasted_iota(jnp.int32, (8, HALF), 0) < 4
    targets = []
    decs = []
    for i in range(3):
        t = jnp.where(chosen, jnp.broadcast_to(tgt_ref[i : i + 1, :][None], shape3), 0.0)
        targets.append(jnp.sum(t, axis=2, keepdims=True))
        decs.append(
            jnp.where(
                low,
                jnp.broadcast_to(dec_ref[i : i + 1, 0:HALF], (8, HALF)),
                jnp.broadcast_to(dec_ref[i : i + 1, HALF:FEAT], (8, HALF)),
            )[None]
        )

    def both_halves(v):
        v = jnp.broadcast_to(jnp.sum(v, axis=2, keepdims=True), (8, 8, R))
        return v + pltpu.roll(v, 4, 1)

    def wide(v):
        return jnp.concatenate([v, v], axis=2)

    def wait_l(e, c):
        l_copy(e, (m + e) % CHIPS).wait_recv()
        return c

    lax.fori_loop(1, CHIPS, wait_l, 0)
    arrived = lr[...].reshape(8, 2, 8, HALF)
    mean = (arrived[:, 0] + arrived[:, 1]) * 0.25
    inverse = wide(lax.rsqrt(both_halves(mean * mean) * (1.0 / FEAT) + FLOOR))
    normed = mean * inverse
    normed_grad = jnp.zeros((8, 8, HALF), F32)
    square = jnp.zeros((8, 8, R), F32)
    dec_rows = []
    for i in range(3):
        residue = both_halves(normed * decs[i]) - targets[i]
        square = square + residue * residue
        res_wide = wide(residue)
        normed_grad = normed_grad + decs[i] * res_wide
        part = jnp.sum(res_wide * normed, axis=0)
        dec_rows.append(jnp.sum(part[0:4], axis=0, keepdims=True))
        dec_rows.append(jnp.sum(part[4:8], axis=0, keepdims=True))
    along = wide(both_halves(normed_grad * normed)) * (1.0 / FEAT)
    pixel_grad = inverse * (normed_grad - normed * along) * 0.25
    lb[...] = pixel_grad.astype(BF16).astype(F32)

    def b_copy(e, src):
        to = (m + e) % CHIPS
        return rc(lb.at[to // 2], br.at[src], s_b.at[to], r_b.at[src], me, to * 2 + h)

    def send_b(e, c):
        b_copy(e, m).start()
        return c

    lax.fori_loop(1, CHIPS, send_b, 0)
    br[m] = lb[m // 2]

    err_row = jnp.sum(jnp.sum(square, axis=0), axis=0, keepdims=True) * 0.5
    dec_rows.append(jnp.concatenate([err_row, err_row], axis=1))
    dec_rows.append(jnp.zeros((1, HALF), F32))
    decall[me] = jnp.concatenate(dec_rows, axis=0)

    def wait_b(e, c):
        b_copy(e, (m + e) % CHIPS).wait_recv()
        return c

    lax.fori_loop(1, CHIPS, wait_b, 0)
    gbuf[me, h] = br[...].reshape(R, HALF).astype(BF16)

    def g_copy(off, k):
        return rc(gbuf.at[k, h], gbuf.at[k, h], s_g.at[off], r_g.at[k], depth_peer(off), lat)

    def pb_copy(d, half):
        return rc(gbuf.at[d, half], gbuf.at[d, half], s_pb.at[d], r_pb.at[d], me, sib)

    def d_copy(off, k):
        return rc(decall.at[k], decall.at[k], s_d.at[off], r_d.at[k], depth_peer(off), lat)

    def send_g(i, c):
        g_copy(offset_of(i), me).start()
        return c

    lax.fori_loop(0, K - 1, send_g, 0)

    def send_d(off, c):
        d_copy(off, me).start()
        return c

    lax.fori_loop(1, K, send_d, 0)

    def take_share(i):
        d = depth_peer(near_offset_of(i))

        @pl.when(i > 0)
        def _():
            g_copy(near_offset_of(i) % K, d).wait_recv()

        pb_copy(d, h).start()

    def back_share(i):
        d = depth_peer(near_offset_of(i))
        pb_copy(d, 1 - h).wait_recv()
        grads = gbuf[d].reshape(2 * R, HALF)
        ray_grad = mm(grads, oh[d], TN)
        terms = jnp.sum(scaled[d].astype(F32) * ray_grad, axis=0, keepdims=True)
        tmall[me, pl.ds(d, 1), :] = terms[:, 0:R] + terms[:, R : 2 * R]
        sc = scl[pl.ds(d, 1), :]
        bld[d] = ray_grad * jnp.concatenate([sc, sc], axis=1)
        weight_grad = [jnp.zeros((8, R), F32) for _ in range(S)]
        for f0 in range(0, FEAT, 64):
            fh = f0 // HALF
            fg = bld[d, f0 - fh * HALF : f0 - fh * HALF + 64, fh * R : (fh + 1) * R]
            for s in range(S):
                part = feats[d, f0 : f0 + 64, s * R : (s + 1) * R].astype(F32) * fg
                weight_grad[s] = weight_grad[s] + jnp.sum(part.reshape(8, 8, R), axis=0)
                feats[d, f0 : f0 + 64, s * R : (s + 1) * R] = (
                    fg * wts[d, s : s + 1, :]
                ).astype(BF16)
        wgs[d] = jnp.concatenate(
            [jnp.sum(weight_grad[s], axis=0, keepdims=True) for s in range(S)], axis=0
        )

    def back_step(i, c):
        take_share(i)

        @pl.when(i >= 1)
        def _():
            back_share(i - 1)

        return c

    lax.fori_loop(0, K, back_step, 0)
    back_share(K - 1)

    def t_copy(off, k):
        return rc(tmall.at[k], tmall.at[k], s_t.at[off], r_t.at[k], depth_peer(off), lat)

    def send_t(off, c):
        t_copy(off, me).start()
        return c

    lax.fori_loop(1, K, send_t, 0)

    def wait_d(off, c):
        d_copy(off, depth_peer(off)).wait_recv()
        return c

    lax.fori_loop(1, K, wait_d, 0)
    dec_sum = decall[0]
    for k in range(1, K):
        dec_sum = dec_sum + decall[k]
    for i in range(3):
        gdec_ref[i : i + 1, 0:HALF] = dec_sum[2 * i : 2 * i + 1]
        gdec_ref[i : i + 1, HALF:FEAT] = dec_sum[2 * i + 1 : 2 * i + 2]
    esend[...] = jnp.broadcast_to(dec_sum[6:7, 0:R], (8, R))
    elat[m] = esend[...]

    def e_copy(e, src):
        to = (m + e) % CHIPS
        return rc(esend, elat.at[src], s_e.at[to], r_e.at[src], me, to * 2 + h)

    def send_e(e, c):
        e_copy(e, m).start()
        return c

    lax.fori_loop(1, CHIPS, send_e, 0)

    g3_ref[...] = jnp.zeros_like(g3_ref)

    def third_step(d, c):
        g3_ref[...] += mm(h2s[d], feats[d], NT)
        return c

    lax.fori_loop(0, K, third_step, 0)

    def wait_e(e, c):
        e_copy(e, (m + e) % CHIPS).wait_recv()
        return c

    lax.fori_loop(1, CHIPS, wait_e, 0)
    err_sum = elat[0]
    for k in range(1, CHIPS):
        err_sum = err_sum + elat[k]
    epsend[...] = err_sum
    ep_copy = rc(epsend, eprec, s_ep, r_ep, me, sib)
    ep_copy.start()

    def wait_t(off, c):
        t_copy(off, depth_peer(off)).wait_recv()
        return c

    lax.fori_loop(1, K, wait_t, 0)
    behind = jnp.zeros((K, R), F32)
    for k in range(K):
        behind = behind + tmall[k] * jnp.where(places[k] > mine, 1.0, 0.0)
    sub2 = lax.broadcasted_iota(jnp.int32, (S, R), 0)
    for d in range(K):
        wg = wgs[d]
        own = wg * wts[d]
        suffix = own
        for sh in (1, 2, 4):
            suffix = suffix + jnp.where(sub2 < S - sh, pltpu.roll(suffix, S - sh, 0), 0.0)
        density_grad = STEP * (wg * expi[d] - (suffix - own) - behind[d : d + 1, :])
        lg = lgs[d]
        sig = 1.0 / (1.0 + jnp.exp(-lg))
        lgrad[d] = (density_grad * sig).astype(BF16).astype(F32)

    g1_ref[...] = jnp.zeros_like(g1_ref)
    g2_ref[...] = jnp.zeros_like(g2_ref)

    def last_step(d, gdens):
        lg = lgrad[d]
        lg8 = jnp.concatenate(
            [jnp.broadcast_to(lg[s : s + 1, :], (8, R)) for s in range(S)], axis=1
        )
        gdens = gdens + mm(lg8.astype(BF16), h2s[d], NT)
        b2 = mm(w3_ref[...], feats[d], NN)
        for s in range(S):
            cols = slice(s * R, (s + 1) * R)
            v = b2[:, cols] + wdb[...] * lg[s : s + 1, :]
            b2s[:, cols] = jnp.where(h2s[d, :, cols].astype(F32) > 0.0, v, 0.0).astype(BF16)
        g2_ref[...] += mm(h1s[d], b2s[...], NT)
        b1 = mm(w2_ref[...], b2s[...], NN)
        b1 = jnp.where(h1s[d].astype(F32) > 0.0, b1, 0.0).astype(BF16)
        g1_ref[...] += mm(take_x(d), b1, NT)
        return gdens

    gdens = lax.fori_loop(0, K, last_step, jnp.zeros((8, HID), F32))
    gd_ref[...] = gdens[0:1]

    ep_copy.wait_recv()
    err_ref[...] = (epsend[0:1, 0:1] + eprec[0:1, 0:1]) * (1.0 / COUNT)

    def end_depth(off, c):
        d = depth_peer(off)
        ds_copy(off, me).wait_send()
        z_copy(d, me).wait_send()
        g_copy(off, me).wait_send()
        d_copy(off, me).wait_send()
        t_copy(off, me).wait_send()
        return c

    lax.fori_loop(1, K, end_depth, 0)

    def end_lateral(e, c):
        l_copy(e, m).wait_send()
        b_copy(e, m).wait_send()
        e_copy(e, m).wait_send()
        return c

    lax.fori_loop(1, CHIPS, end_lateral, 0)

    def end_pair(d, c):
        pf_copy(d).wait_send()
        pb_copy(d, h).wait_send()
        return c

    lax.fori_loop(0, K, end_pair, 0)
    ep_copy.wait_send()


def body(samples, w_first, w_second, w_third, w_density, decoder, depth_order, ray_slot, target):
    vmem = pl.BlockSpec(memory_space=pltpu.VMEM)
    dma = pltpu.SemaphoreType.DMA
    v = pltpu.VMEM
    outs = pl.pallas_call(
        kernel,
        name="step",
        out_shape=(
            jax.ShapeDtypeStruct((ENC, HID), F32),
            jax.ShapeDtypeStruct((HID, HID), F32),
            jax.ShapeDtypeStruct((HID, FEAT), F32),
            jax.ShapeDtypeStruct((1, HID), F32),
            jax.ShapeDtypeStruct((3, FEAT), F32),
            jax.ShapeDtypeStruct((1, 1), F32),
        ),
        in_specs=[vmem] * 6 + [pl.BlockSpec(memory_space=pltpu.SMEM)] + [vmem] * 2,
        out_specs=(vmem,) * 6,
        scratch_shapes=[
            v((HID, ENC), BF16),
            v((HID, HID), BF16),
            v((FEAT, HID), BF16),
            v((HID, R), F32),
            v((K, HID, W), BF16),
            v((K, HID, W), BF16),
            v((K, FEAT, W), BF16),
            v((K, S, R), F32),
            v((K, S, R), F32),
            v((K, S, R), F32),
            v((K, HALF, 2 * R), F32),
            v((K, R), F32),
            v((K, HALF, 2 * R), BF16),
            v((K, 2 * R, 2 * R), BF16),
            v((K, 2, R, HALF), BF16),
            v((K, R, HALF), BF16),
            v((K, R, HALF), BF16),
            v((K, R, HALF), BF16),
            v((CHIPS, 8, HALF), F32),
            v((CHIPS, 8, HALF), F32),
            v((8, 8, HALF), F32),
            v((CHIPS, 8, HALF), F32),
            v((K, 2, R, HALF), BF16),
            v((K, K, R), F32),
            v((K, K, R), F32),
            v((K, S, R), F32),
            v((K, S, R), F32),
            v((HID, W), BF16),
            v((K, 8, HALF), F32),
            v((8, R), F32),
            v((CHIPS, 8, R), F32),
            v((8, R), F32),
            v((8, R), F32),
            dma((K,)), dma((K,)),
            dma((K,)), dma((K,)),
            dma((K,)), dma((K,)),
            dma((CHIPS,)), dma((CHIPS,)),
            dma((CHIPS,)), dma((CHIPS,)),
            dma((K,)), dma((K,)),
            dma((K,)), dma((K,)),
            dma((K,)), dma((K,)),
            dma((K,)), dma((K,)),
            dma((CHIPS,)), dma((CHIPS,)),
            dma(()), dma(()),
        ],
        compiler_params=pltpu.CompilerParams(
            collective_id=0, has_side_effects=True, vmem_limit_bytes=58 * 1024 * 1024
        ),
    )(
        samples[0, 0],
        w_first[0, 0],
        w_second[0, 0],
        w_third[0, 0],
        w_density[0],
        decoder[0],
        depth_order,
        ray_slot,
        target[0],
    )
    return (
        outs[0][None, None],
        outs[1][None, None],
        outs[2][None, None],
        outs[3][None],
        outs[4][None],
        outs[5][0, 0],
    )


def solution(mesh):
    placed = (
        P("depth", "lateral", None, None),
        P("depth", "lateral", None, None),
        P("depth", "lateral", None, None),
        P("depth", "lateral", None, None),
        P("depth", "lateral", None),
        P("lateral", None, None),
        P("lateral", None),
        P("lateral", None),
        P("lateral", None, "depth"),
    )
    return jax.shard_map(
        body,
        mesh=mesh,
        in_specs=placed,
        out_specs=(
            P("depth", "lateral", None, None),
            P("depth", "lateral", None, None),
            P("depth", "lateral", None, None),
            P("depth", "lateral", None),
            P("lateral", None, None),
            P(),
        ),
        check_vma=False,
    )
```

```python
import jax
import jax.numpy as jnp
from jax import lax
from jax.experimental import pallas as pl
from jax.experimental.pallas import tpu as pltpu
from jax.sharding import PartitionSpec as P

MESH = pl.DeviceIdType.MESH
F32 = jnp.float32
BF16 = jnp.bfloat16

ENC, HID, FEAT = 64, 256, 512
S = 8
K = 8
R = 128
CHIPS = 16
W = S * R
HALF = FEAT // 2
STEP = 0.04
FLOOR = 1e-05
COUNT = 24576.0
LAG = 3
LATE = 4

NN = (((1,), (0,)), ((), ()))
NT = (((1,), (1,)), ((), ()))
TN = (((0,), (0,)), ((), ()))


def mm(a, b, dims):
    return lax.dot_general(a, b, dims, preferred_element_type=F32)


def offset_of(i):
    return 4 + ((i + 1) // 2) * (1 - 2 * (i % 2))


def near_offset_of(i):
    return ((i + 1) // 2) * (2 * (i % 2) - 1) + 8


def kernel(
    x_ref, w1_ref, w2_ref, w3_ref, wd_ref, dec_ref, order_ref, slot_ref, tgt_ref,
    g1_ref, g2_ref, g3_ref, gd_ref, gdec_ref, err_ref,
    w1t, w2t, w3t, wdb, h1s, h2s, feats, lgs, wts, expi, bld, scl, scaled, oh,
    pfull, prec, zsend, zrecv, lt, lr, lb, br, gbuf, dsall, tmall, wgs, lgrad, b2s, b2p,
    decall, esend, elat, epsend, eprec,
    s_ds, r_ds, s_pf, r_pf, s_z, r_z, s_l, r_l, s_b, r_b, s_g, r_g, s_pb, r_pb,
    s_t, r_t, s_d, r_d, s_e, r_e, s_ep, r_ep,
):
    me = lax.axis_index("depth")
    lat = lax.axis_index("lateral")
    h = lat % 2
    m = lat // 2
    sib = lat + 1 - 2 * h

    def depth_peer(off):
        return (me + off) % K

    def rc(src, dst, ssem, rsem, z, l):
        return pltpu.make_async_remote_copy(
            src_ref=src, dst_ref=dst, send_sem=ssem, recv_sem=rsem,
            device_id=(z, l), device_id_type=MESH,
        )

    barrier = pltpu.get_barrier_semaphore()

    def greet_depth(e, c):
        pl.semaphore_signal(barrier, inc=1, device_id=((me + e) % K, lat), device_id_type=MESH)
        return c

    def greet_lateral(e, c):
        pl.semaphore_signal(
            barrier, inc=1, device_id=(me, ((m + e) % CHIPS) * 2 + h), device_id_type=MESH
        )
        return c

    lax.fori_loop(1, K, greet_depth, 0)
    lax.fori_loop(1, CHIPS, greet_lateral, 0)
    pl.semaphore_signal(barrier, inc=1, device_id=(me, sib), device_id_type=MESH)

    w1t[...] = w1_ref[...].T
    w2t[...] = w2_ref[...].T
    w3t[...] = w3_ref[...].T
    wd8 = jnp.broadcast_to(wd_ref[...], (8, HID))
    wdb[...] = jnp.broadcast_to(wd_ref[...].astype(F32), (R, HID)).T

    def take_x(d):
        return jnp.concatenate(
            [x_ref[:, pl.ds(pl.multiple_of(s * (K * R) + d * R, R), R)] for s in range(S)], axis=1
        )

    def first_pass(d, c):
        x = take_x(d)
        h1s[d] = jnp.maximum(mm(w1t[...], x, NN), 0.0).astype(BF16)
        h2s[d] = jnp.maximum(mm(w2t[...], h1s[d], NN), 0.0).astype(BF16)
        lg = mm(wd8, h2s[d], NN)
        lgs[d] = jnp.concatenate(
            [lg[s : s + 1, s * R : (s + 1) * R] for s in range(S)], axis=0
        )
        return c

    lax.fori_loop(0, K, first_pass, 0)

    sub = lax.broadcasted_iota(jnp.int32, (K, S, R), 1)
    logits = lgs[...]
    density = jnp.maximum(logits, 0.0) + jnp.log1p(jnp.exp(-jnp.abs(logits)))
    inc = density
    for sh in (1, 2, 4):
        inc = inc + jnp.where(sub >= sh, pltpu.roll(inc, sh, 1), 0.0)
    wts[...] = jnp.exp(-STEP * (inc - density)) * (1.0 - jnp.exp(-STEP * density))
    expi[...] = jnp.exp(-STEP * inc)
    dsall[me] = STEP * jnp.concatenate([inc[d, S - 1 : S, :] for d in range(K)], axis=0)

    pl.semaphore_wait(barrier, K - 1 + CHIPS - 1 + 1)

    def ds_copy(off, k):
        return rc(dsall.at[k], dsall.at[k], s_ds.at[off], r_ds.at[k], depth_peer(off), lat)

    def send_ds(off, c):
        ds_copy(off, me).start()
        return c

    lax.fori_loop(1, K, send_ds, 0)

    row = lax.broadcasted_iota(jnp.int32, (2 * R, R), 0)
    code = (((row // 8) % CHIPS) * 2 + row // R) * 4 + row % 4
    code_lo = jnp.where((row // 4) % 2 == 0, code, -1)
    code_hi = jnp.where((row // 4) % 2 == 1, code, -1)

    def one_hot(d, c):
        slots = slot_ref[:, pl.ds(pl.multiple_of(d * R, R), R)]
        oh[d] = jnp.concatenate(
            [
                jnp.where(code_lo == slots, 1.0, 0.0).astype(BF16),
                jnp.where(code_hi == slots, 1.0, 0.0).astype(BF16),
            ],
            axis=1,
        )
        return c

    lax.fori_loop(0, K, one_hot, 0)

    def second_pass(d, c):
        feats[d] = mm(w3t[...], h2s[d], NN).astype(BF16)
        for f0 in range(0, FEAT, 64):
            total = jnp.zeros((64, R), F32)
            for s in range(S):
                total = total + feats[d, f0 : f0 + 64, s * R : (s + 1) * R].astype(F32) * wts[
                    d, s : s + 1, :
                ]
            fh = f0 // HALF
            bld[d, f0 - fh * HALF : f0 - fh * HALF + 64, fh * R : (fh + 1) * R] = total
        return c

    lax.fori_loop(0, K, second_pass, 0)

    places = []
    mine = jnp.int32(0)
    for k in range(K):
        place = jnp.int32(0)
        for p in range(K):
            place = place + jnp.where(order_ref[0, p] == k, p, 0)
        places.append(place)
    for p in range(K):
        mine = mine + jnp.where(order_ref[0, p] == me, p, 0)

    def wait_ds(off, c):
        ds_copy(off, depth_peer(off)).wait_recv()
        return c

    lax.fori_loop(1, K, wait_ds, 0)
    before = jnp.zeros((K, R), F32)
    for k in range(K):
        before = before + dsall[k] * jnp.where(places[k] < mine, 1.0, 0.0)
    scl[...] = jnp.exp(-before)

    def pf_copy(d):
        return rc(pfull.at[d, 1 - h], prec.at[d], s_pf.at[d], r_pf.at[d], me, sib)

    def z_copy(d, k):
        return rc(zsend.at[d], zrecv.at[k], s_z.at[d], r_z.at[k], d, lat)

    def make_scaled(d):
        sc = scl[pl.ds(d, 1), :]
        sc = jnp.concatenate([sc, sc], axis=1)
        scaled[d] = (bld[d] * sc).astype(BF16)
        placed = mm(oh[d], scaled[d], NT).astype(BF16)
        pfull[d, 0] = placed[0:R]
        pfull[d, 1] = placed[R : 2 * R]
        pf_copy(d).start()

    def pair_sum(d):
        pf_copy(d).wait_recv()
        return (pfull[d, h].astype(F32) + prec[d].astype(F32)).astype(BF16)

    def send_share(i):
        d = depth_peer(offset_of(i))
        zsend[d] = pair_sum(d)
        z_copy(d, me).start()

    def scaled_step(i, c):
        make_scaled(depth_peer(offset_of(i)))

        @pl.when(i >= LAG)
        def _():
            send_share(i - LAG)

        return c

    lax.fori_loop(0, K, scaled_step, 0)
    for i in range(K - LAG, K - 1):
        send_share(i)
    zrecv[me] = pair_sum(me)

    def wait_z(off, c):
        z_copy(me, depth_peer(off)).wait_recv()
        return c

    lax.fori_loop(1, K, wait_z, 0)
    total = zrecv[0].astype(F32)
    for k in range(1, K):
        total = total + zrecv[k].astype(F32)
    lt[...] = total.reshape(CHIPS, 8, HALF)

    def l_copy(e, src):
        to = (m + e) % CHIPS
        return rc(lt.at[to], lr.at[src], s_l.at[to], r_l.at[src], me, to * 2 + h)

    def send_l(e, c):
        l_copy(e, m).start()
        return c

    lax.fori_loop(1, CHIPS, send_l, 0)
    lr[m] = lt[m]

    shape3 = (8, 8, 32)
    grp = lax.broadcasted_iota(jnp.int32, shape3, 0)
    rowq = lax.broadcasted_iota(jnp.int32, shape3, 1) % 4
    pix = lax.broadcasted_iota(jnp.int32, shape3, 2)
    chosen = pix == rowq * 8 + grp
    low = lax.broadcasted_iota(jnp.int32, (8, HALF), 0) < 4
    targets = []
    decs = []
    for i in range(3):
        t = jnp.where(chosen, jnp.broadcast_to(tgt_ref[i][None], shape3), 0.0)
        targets.append(jnp.sum(t, axis=2, keepdims=True))
        decs.append(
            jnp.where(
                low,
                jnp.broadcast_to(dec_ref[i, :, 0:HALF], (8, HALF)),
                jnp.broadcast_to(dec_ref[i, :, HALF:FEAT], (8, HALF)),
            )[None]
        )

    def both_halves(v):
        v = jnp.broadcast_to(jnp.sum(v, axis=2, keepdims=True), (8, 8, R))
        return v + pltpu.roll(v, 4, 1)

    def wide(v):
        return jnp.concatenate([v, v], axis=2)

    def wait_l(e, c):
        l_copy(e, (m + e) % CHIPS).wait_recv()
        return c

    lax.fori_loop(1, CHIPS, wait_l, 0)
    arrived = lr[...].reshape(8, 2, 8, HALF)
    mean = (arrived[:, 0] + arrived[:, 1]) * 0.25
    inverse = wide(lax.rsqrt(both_halves(mean * mean) * (1.0 / FEAT) + FLOOR))
    normed = mean * inverse
    normed_grad = jnp.zeros((8, 8, HALF), F32)
    square = jnp.zeros((8, 8, R), F32)
    dec_rows = []
    for i in range(3):
        residue = both_halves(normed * decs[i]) - targets[i]
        square = square + residue * residue
        res_wide = wide(residue)
        normed_grad = normed_grad + decs[i] * res_wide
        part = jnp.sum(res_wide * normed, axis=0)
        dec_rows.append(jnp.sum(part[0:4], axis=0, keepdims=True))
        dec_rows.append(jnp.sum(part[4:8], axis=0, keepdims=True))
    along = wide(both_halves(normed_grad * normed)) * (1.0 / FEAT)
    pixel_grad = inverse * (normed_grad - normed * along) * 0.25
    lb[...] = pixel_grad.astype(BF16).astype(F32)

    def b_copy(e, src):
        to = (m + e) % CHIPS
        return rc(lb.at[to // 2], br.at[src], s_b.at[to], r_b.at[src], me, to * 2 + h)

    def send_b(e, c):
        b_copy(e, m).start()
        return c

    lax.fori_loop(1, CHIPS, send_b, 0)
    br[m] = lb[m // 2]

    err_row = jnp.sum(jnp.sum(square, axis=0), axis=0, keepdims=True) * 0.5
    dec_rows.append(jnp.concatenate([err_row, err_row], axis=1))
    dec_rows.append(jnp.zeros((1, HALF), F32))
    decall[me] = jnp.concatenate(dec_rows, axis=0)

    def wait_b(e, c):
        b_copy(e, (m + e) % CHIPS).wait_recv()
        return c

    lax.fori_loop(1, CHIPS, wait_b, 0)
    gbuf[me, h] = br[...].reshape(R, HALF).astype(BF16)

    def g_copy(off, k):
        return rc(gbuf.at[k, h], gbuf.at[k, h], s_g.at[off], r_g.at[k], depth_peer(off), lat)

    def pb_copy(d, half):
        return rc(gbuf.at[d, half], gbuf.at[d, half], s_pb.at[d], r_pb.at[d], me, sib)

    def d_copy(off, k):
        return rc(decall.at[k], decall.at[k], s_d.at[off], r_d.at[k], depth_peer(off), lat)

    def send_g(i, c):
        g_copy(near_offset_of(i) % K, me).start()
        return c

    lax.fori_loop(1, K, send_g, 0)

    def send_d(off, c):
        d_copy(off, me).start()
        return c

    lax.fori_loop(1, K, send_d, 0)

    def take_share(i):
        d = depth_peer(near_offset_of(i))

        @pl.when(i > 0)
        def _():
            g_copy(near_offset_of(i) % K, d).wait_recv()

        pb_copy(d, h).start()

    def back_share(i):
        d = depth_peer(near_offset_of(i))
        pb_copy(d, 1 - h).wait_recv()
        grads = gbuf[d].reshape(2 * R, HALF)
        ray_grad = mm(grads, oh[d], TN)
        terms = jnp.sum(scaled[d].astype(F32) * ray_grad, axis=0, keepdims=True)
        tmall[me, pl.ds(d, 1), :] = terms[:, 0:R] + terms[:, R : 2 * R]
        sc = scl[pl.ds(d, 1), :]
        bld[d] = ray_grad * jnp.concatenate([sc, sc], axis=1)
        weight_grad = [jnp.zeros((8, R), F32) for _ in range(S)]
        for f0 in range(0, FEAT, 64):
            fh = f0 // HALF
            fg = bld[d, f0 - fh * HALF : f0 - fh * HALF + 64, fh * R : (fh + 1) * R]
            for s in range(S):
                part = feats[d, f0 : f0 + 64, s * R : (s + 1) * R].astype(F32) * fg
                weight_grad[s] = weight_grad[s] + jnp.sum(part.reshape(8, 8, R), axis=0)
                feats[d, f0 : f0 + 64, s * R : (s + 1) * R] = (
                    fg * wts[d, s : s + 1, :]
                ).astype(BF16)
        wgs[d] = jnp.concatenate(
            [jnp.sum(weight_grad[s], axis=0, keepdims=True) for s in range(S)], axis=0
        )

    def third_share(i):
        d = depth_peer(near_offset_of(i))
        g3_ref[...] += mm(h2s[d], feats[d], NT)
        b2p[d] = mm(w3_ref[...], feats[d], NN)

    g3_ref[...] = jnp.zeros_like(g3_ref)

    def back_step(i, c):
        @pl.when(i >= LATE + 1)
        def _():
            third_share(i - 1 - LATE)

        take_share(i)

        @pl.when(i >= 1)
        def _():
            back_share(i - 1)

        return c

    lax.fori_loop(0, K, back_step, 0)
    third_share(K - 1 - LATE)
    back_share(K - 1)

    def t_copy(off, k):
        return rc(tmall.at[k], tmall.at[k], s_t.at[off], r_t.at[k], depth_peer(off), lat)

    def send_t(off, c):
        t_copy(off, me).start()
        return c

    lax.fori_loop(1, K, send_t, 0)

    def wait_d(off, c):
        d_copy(off, depth_peer(off)).wait_recv()
        return c

    lax.fori_loop(1, K, wait_d, 0)
    dec_sum = decall[0]
    for k in range(1, K):
        dec_sum = dec_sum + decall[k]
    for i in range(3):
        gdec_ref[i, :, 0:HALF] = dec_sum[2 * i : 2 * i + 1]
        gdec_ref[i, :, HALF:FEAT] = dec_sum[2 * i + 1 : 2 * i + 2]
    esend[...] = jnp.broadcast_to(dec_sum[6:7, 0:R], (8, R))
    elat[m] = esend[...]

    def e_copy(e, src):
        to = (m + e) % CHIPS
        return rc(esend, elat.at[src], s_e.at[to], r_e.at[src], me, to * 2 + h)

    def send_e(e, c):
        e_copy(e, m).start()
        return c

    lax.fori_loop(1, CHIPS, send_e, 0)

    def third_step(i, c):
        third_share(i)
        return c

    lax.fori_loop(K - LATE, K, third_step, 0)

    def wait_e(e, c):
        e_copy(e, (m + e) % CHIPS).wait_recv()
        return c

    lax.fori_loop(1, CHIPS, wait_e, 0)
    err_sum = elat[0]
    for k in range(1, CHIPS):
        err_sum = err_sum + elat[k]
    epsend[...] = err_sum
    ep_copy = rc(epsend, eprec, s_ep, r_ep, me, sib)
    ep_copy.start()

    def wait_t(off, c):
        t_copy(off, depth_peer(off)).wait_recv()
        return c

    lax.fori_loop(1, K, wait_t, 0)
    behind = jnp.zeros((K, R), F32)
    for k in range(K):
        behind = behind + tmall[k] * jnp.where(places[k] > mine, 1.0, 0.0)
    sub2 = lax.broadcasted_iota(jnp.int32, (S, R), 0)
    for d in range(K):
        wg = wgs[d]
        own = wg * wts[d]
        suffix = own
        for sh in (1, 2, 4):
            suffix = suffix + jnp.where(sub2 < S - sh, pltpu.roll(suffix, S - sh, 0), 0.0)
        density_grad = STEP * (wg * expi[d] - (suffix - own) - behind[d : d + 1, :])
        lg = lgs[d]
        sig = 1.0 / (1.0 + jnp.exp(-lg))
        lgrad[d] = (density_grad * sig).astype(BF16).astype(F32)

    g1_ref[...] = jnp.zeros_like(g1_ref)
    g2_ref[...] = jnp.zeros_like(g2_ref)

    def last_step(d, gdens):
        lg = lgrad[d]
        lg8 = jnp.concatenate(
            [jnp.broadcast_to(lg[s : s + 1, :], (8, R)) for s in range(S)], axis=1
        )
        gdens = gdens + mm(lg8.astype(BF16), h2s[d], NT)
        for s in range(S):
            cols = slice(s * R, (s + 1) * R)
            v = b2p[d, :, cols] + wdb[...] * lg[s : s + 1, :]
            b2s[:, cols] = jnp.where(h2s[d, :, cols].astype(F32) > 0.0, v, 0.0).astype(BF16)
        g2_ref[...] += mm(h1s[d], b2s[...], NT)
        b1 = mm(w2_ref[...], b2s[...], NN)
        b1 = jnp.where(h1s[d].astype(F32) > 0.0, b1, 0.0).astype(BF16)
        g1_ref[...] += mm(take_x(d), b1, NT)
        return gdens

    gdens = lax.fori_loop(0, K, last_step, jnp.zeros((8, HID), F32))
    gd_ref[...] = gdens[0:1]

    ep_copy.wait_recv()
    err_ref[...] = (epsend[0:1, 0:1] + eprec[0:1, 0:1]) * (1.0 / COUNT)

    def end_depth(off, c):
        d = depth_peer(off)
        ds_copy(off, me).wait_send()
        z_copy(d, me).wait_send()
        g_copy(off, me).wait_send()
        d_copy(off, me).wait_send()
        t_copy(off, me).wait_send()
        return c

    lax.fori_loop(1, K, end_depth, 0)

    def end_lateral(e, c):
        l_copy(e, m).wait_send()
        b_copy(e, m).wait_send()
        e_copy(e, m).wait_send()
        return c

    lax.fori_loop(1, CHIPS, end_lateral, 0)

    def end_pair(d, c):
        pf_copy(d).wait_send()
        pb_copy(d, h).wait_send()
        return c

    lax.fori_loop(0, K, end_pair, 0)
    ep_copy.wait_send()


def put_out(*refs):
    for i in range(6):
        refs[6 + i][...] = refs[i][...]


def body(samples, w_first, w_second, w_third, w_density, decoder, depth_order, ray_slot, target):
    vmem = pl.BlockSpec(memory_space=pltpu.VMEM)
    dma = pltpu.SemaphoreType.DMA
    v = pltpu.VMEM
    results = ((ENC, HID), (HID, HID), (HID, FEAT), (1, HID), (3, 1, FEAT), (1, 1))
    outs = pl.pallas_call(
        kernel,
        name="step",
        out_shape=tuple(pltpu.VMEM(shape, F32) for shape in results),
        in_specs=[vmem] * 6 + [pl.BlockSpec(memory_space=pltpu.SMEM)] + [vmem] * 2,
        out_specs=(vmem,) * 6,
        scratch_shapes=[
            v((HID, ENC), BF16),
            v((HID, HID), BF16),
            v((FEAT, HID), BF16),
            v((HID, R), F32),
            v((K, HID, W), BF16),
            v((K, HID, W), BF16),
            v((K, FEAT, W), BF16),
            v((K, S, R), F32),
            v((K, S, R), F32),
            v((K, S, R), F32),
            v((K, HALF, 2 * R), F32),
            v((K, R), F32),
            v((K, HALF, 2 * R), BF16),
            v((K, 2 * R, 2 * R), BF16),
            v((K, 2, R, HALF), BF16),
            v((K, R, HALF), BF16),
            v((K, R, HALF), BF16),
            v((K, R, HALF), BF16),
            v((CHIPS, 8, HALF), F32),
            v((CHIPS, 8, HALF), F32),
            v((8, 8, HALF), F32),
            v((CHIPS, 8, HALF), F32),
            v((K, 2, R, HALF), BF16),
            v((K, K, R), F32),
            v((K, K, R), F32),
            v((K, S, R), F32),
            v((K, S, R), F32),
            v((HID, W), BF16),
            v((K, HID, W), F32),
            v((K, 8, HALF), F32),
            v((8, R), F32),
            v((CHIPS, 8, R), F32),
            v((8, R), F32),
            v((8, R), F32),
            dma((K,)), dma((K,)),
            dma((K,)), dma((K,)),
            dma((K,)), dma((K,)),
            dma((CHIPS,)), dma((CHIPS,)),
            dma((CHIPS,)), dma((CHIPS,)),
            dma((K,)), dma((K,)),
            dma((K,)), dma((K,)),
            dma((K,)), dma((K,)),
            dma((K,)), dma((K,)),
            dma((CHIPS,)), dma((CHIPS,)),
            dma(()), dma(()),
        ],
        compiler_params=pltpu.CompilerParams(
            collective_id=0, has_side_effects=True, vmem_limit_bytes=58 * 1024 * 1024
        ),
    )(
        samples[0, 0],
        w_first[0, 0],
        w_second[0, 0],
        w_third[0, 0],
        w_density[0],
        jnp.transpose(decoder, (1, 0, 2)),
        depth_order,
        ray_slot,
        jnp.transpose(target, (1, 0, 2)),
    )
    outs = pl.pallas_call(
        put_out,
        name="put_out",
        out_shape=tuple(jax.ShapeDtypeStruct(shape, F32) for shape in results),
        in_specs=[vmem] * 6,
        out_specs=(vmem,) * 6,
    )(*[pltpu.with_memory_space_constraint(o, pltpu.VMEM) for o in outs])
    return (
        outs[0][None, None],
        outs[1][None, None],
        outs[2][None, None],
        outs[3][None],
        jnp.transpose(outs[4], (1, 0, 2)),
        outs[5][0, 0],
    )


def solution(mesh):
    placed = (
        P("depth", "lateral", None, None),
        P("depth", "lateral", None, None),
        P("depth", "lateral", None, None),
        P("depth", "lateral", None, None),
        P("depth", "lateral", None),
        P("lateral", None, None),
        P("lateral", None),
        P("lateral", None),
        P("lateral", None, "depth"),
    )
    return jax.shard_map(
        body,
        mesh=mesh,
        in_specs=placed,
        out_specs=(
            P("depth", "lateral", None, None),
            P("depth", "lateral", None, None),
            P("depth", "lateral", None, None),
            P("depth", "lateral", None),
            P("lateral", None, None),
            P(),
        ),
        check_vma=False,
    )
```

```python
import jax
import jax.numpy as jnp
from jax import lax
from jax.experimental import pallas as pl
from jax.experimental.pallas import tpu as pltpu
from jax.sharding import PartitionSpec as P

MESH = pl.DeviceIdType.MESH
F32 = jnp.float32
BF16 = jnp.bfloat16

ENC, HID, FEAT = 64, 256, 512
S = 8
K = 8
R = 128
CHIPS = 16
G = 8
W = S * R
HALF = FEAT // 2
STEP = 0.04
FLOOR = 1e-05
COUNT = 24576.0
LATE = 6

NN = (((1,), (0,)), ((), ()))
NT = (((1,), (1,)), ((), ()))
TN = (((0,), (0,)), ((), ()))


def mm(a, b, dims):
    return lax.dot_general(a, b, dims, preferred_element_type=F32)


def offset_of(i):
    return 4 + ((i + 1) // 2) * (1 - 2 * (i % 2))


def near_offset_of(i):
    return ((i + 1) // 2) * (2 * (i % 2) - 1) + 8


def kernel(
    x_ref, w1_ref, w2_ref, w3_ref, wd_ref, dec_ref, order_ref, slot_ref, tgt_ref,
    g1_ref, g2_ref, g3_ref, gd_ref, gdec_ref, err_ref,
    w1t, w2t, w3t, wdb, h1s, h2s, feats, lgs, wts, expi, bld, scl, scaled, oh,
    pfull, prec, ysend, yrec, zsend, zrecv, lt, lr, lb, br, gbuf, dsall, tmall, wgs, lgrad, b2s, b2p,
    decall, esend, elat, epsend, eprec,
    s_ds, r_ds, s_pf, r_pf, s_y, r_y, s_z, r_z, s_l, r_l, s_b, r_b, s_g, r_g, s_n, r_n, s_pb, r_pb,
    s_t, r_t, s_d, r_d, s_e, r_e, s_ep, r_ep,
):
    me = lax.axis_index("depth")
    lat = lax.axis_index("lateral")
    h = lat % 2
    m = lat // 2
    sib = lat + 1 - 2 * h
    g = m // 2
    st = ((m % 4 + 1) // 2) % 2
    near = (m + 1 - 2 * (m % 2)) * 2 + h

    def chip_of(s, i):
        return (i // 2) * 4 + 2 * (i % 2) + (s + i) % 2

    def depth_peer(off):
        return (me + off) % K

    def rc(src, dst, ssem, rsem, z, l):
        return pltpu.make_async_remote_copy(
            src_ref=src, dst_ref=dst, send_sem=ssem, recv_sem=rsem,
            device_id=(z, l), device_id_type=MESH,
        )

    barrier = pltpu.get_barrier_semaphore()

    def greet_depth(e, c):
        pl.semaphore_signal(barrier, inc=1, device_id=((me + e) % K, lat), device_id_type=MESH)
        return c

    def greet_lateral(e, c):
        pl.semaphore_signal(
            barrier, inc=1, device_id=(me, ((m + e) % CHIPS) * 2 + h), device_id_type=MESH
        )
        return c

    lax.fori_loop(1, K, greet_depth, 0)
    lax.fori_loop(1, CHIPS, greet_lateral, 0)
    pl.semaphore_signal(barrier, inc=1, device_id=(me, sib), device_id_type=MESH)

    w1t[...] = w1_ref[...].T
    w2t[...] = w2_ref[...].T
    w3t[...] = w3_ref[...].T
    wd8 = jnp.broadcast_to(wd_ref[...], (8, HID))
    wdb[...] = jnp.broadcast_to(wd_ref[...].astype(F32), (R, HID)).T

    def take_x(d):
        return jnp.concatenate(
            [x_ref[:, pl.ds(pl.multiple_of(s * (K * R) + d * R, R), R)] for s in range(S)], axis=1
        )

    def first_pass(d, c):
        x = take_x(d)
        h1s[d] = jnp.maximum(mm(w1t[...], x, NN), 0.0).astype(BF16)
        h2s[d] = jnp.maximum(mm(w2t[...], h1s[d], NN), 0.0).astype(BF16)
        lg = mm(wd8, h2s[d], NN)
        lgs[d] = jnp.concatenate(
            [lg[s : s + 1, s * R : (s + 1) * R] for s in range(S)], axis=0
        )
        return c

    lax.fori_loop(0, K, first_pass, 0)

    sub = lax.broadcasted_iota(jnp.int32, (K, S, R), 1)
    logits = lgs[...]
    density = jnp.maximum(logits, 0.0) + jnp.log1p(jnp.exp(-jnp.abs(logits)))
    inc = density
    for sh in (1, 2, 4):
        inc = inc + jnp.where(sub >= sh, pltpu.roll(inc, sh, 1), 0.0)
    wts[...] = jnp.exp(-STEP * (inc - density)) * (1.0 - jnp.exp(-STEP * density))
    expi[...] = jnp.exp(-STEP * inc)
    dsall[me] = STEP * jnp.concatenate([inc[d, S - 1 : S, :] for d in range(K)], axis=0)

    pl.semaphore_wait(barrier, K - 1 + CHIPS - 1 + 1)

    def ds_copy(off, k):
        return rc(dsall.at[k], dsall.at[k], s_ds.at[off], r_ds.at[k], depth_peer(off), lat)

    def send_ds(off, c):
        ds_copy(off, me).start()
        return c

    lax.fori_loop(1, K, send_ds, 0)

    row = lax.broadcasted_iota(jnp.int32, (2 * R, R), 0)
    code = (chip_of((row // 64) % 2, (row // 8) % G) * 2 + row // R) * 4 + row % 4
    code_lo = jnp.where((row // 4) % 2 == 0, code, -1)
    code_hi = jnp.where((row // 4) % 2 == 1, code, -1)

    def one_hot(d, c):
        slots = slot_ref[:, pl.ds(pl.multiple_of(d * R, R), R)]
        oh[d] = jnp.concatenate(
            [
                jnp.where(code_lo == slots, 1.0, 0.0).astype(BF16),
                jnp.where(code_hi == slots, 1.0, 0.0).astype(BF16),
            ],
            axis=1,
        )
        return c

    lax.fori_loop(0, K, one_hot, 0)

    def second_pass(d, c):
        feats[d] = mm(w3t[...], h2s[d], NN).astype(BF16)
        for f0 in range(0, FEAT, 64):
            total = jnp.zeros((64, R), F32)
            for s in range(S):
                total = total + feats[d, f0 : f0 + 64, s * R : (s + 1) * R].astype(F32) * wts[
                    d, s : s + 1, :
                ]
            fh = f0 // HALF
            bld[d, f0 - fh * HALF : f0 - fh * HALF + 64, fh * R : (fh + 1) * R] = total
        return c

    lax.fori_loop(0, K, second_pass, 0)

    places = []
    mine = jnp.int32(0)
    for k in range(K):
        place = jnp.int32(0)
        for p in range(K):
            place = place + jnp.where(order_ref[0, p] == k, p, 0)
        places.append(place)
    for p in range(K):
        mine = mine + jnp.where(order_ref[0, p] == me, p, 0)

    def wait_ds(off, c):
        ds_copy(off, depth_peer(off)).wait_recv()
        return c

    lax.fori_loop(1, K, wait_ds, 0)
    before = jnp.zeros((K, R), F32)
    for k in range(K):
        before = before + dsall[k] * jnp.where(places[k] < mine, 1.0, 0.0)
    scl[...] = jnp.exp(-before)

    def pf_copy(d):
        return rc(pfull.at[d, 1 - h], prec.at[d], s_pf.at[d], r_pf.at[d], me, sib)

    def y_copy(d):
        return rc(ysend.at[d], yrec.at[d], s_y.at[d], r_y.at[d], me, near)

    def z_copy(d, k):
        return rc(zsend.at[d], zrecv.at[k], s_z.at[d], r_z.at[k], d, lat)

    def make_scaled(i, c):
        d = depth_peer(offset_of(i))
        sc = scl[pl.ds(d, 1), :]
        sc = jnp.concatenate([sc, sc], axis=1)
        scaled[d] = (bld[d] * sc).astype(BF16)
        placed = mm(oh[d], scaled[d], NT).astype(BF16)
        for half in range(2):
            for s in range(2):
                r0 = half * R + s * 64
                pfull[d, half, s] = placed[r0 : r0 + 64]
        pf_copy(d).start()
        return c

    lax.fori_loop(0, K, make_scaled, 0)

    def pair_sum(d, s):
        return pfull[d, h, s].astype(F32) + prec[d, s].astype(F32)

    def send_near(i, c):
        d = depth_peer(offset_of(i))
        pf_copy(d).wait_recv()
        ysend[d] = pair_sum(d, 1 - st).astype(BF16)
        y_copy(d).start()
        return c

    lax.fori_loop(0, K, send_near, 0)

    def group_sum(d):
        y_copy(d).wait_recv()
        return (pair_sum(d, st) + yrec[d].astype(F32)).astype(BF16)

    def send_share(i, c):
        d = depth_peer(offset_of(i))
        zsend[d] = group_sum(d)
        z_copy(d, me).start()
        return c

    lax.fori_loop(0, K - 1, send_share, 0)
    zrecv[me] = group_sum(me)

    def wait_z(off, c):
        z_copy(me, depth_peer(off)).wait_recv()
        return c

    lax.fori_loop(1, K, wait_z, 0)
    total = zrecv[0].astype(F32)
    for k in range(1, K):
        total = total + zrecv[k].astype(F32)
    lt[...] = total.reshape(G, 8, HALF)

    def l_copy(e, src):
        to = (g + e) % G
        return rc(lt.at[to], lr.at[src], s_l.at[to], r_l.at[src], me, chip_of(st, to) * 2 + h)

    def send_l(e, c):
        l_copy(e, g).start()
        return c

    lax.fori_loop(1, G, send_l, 0)
    lr[g] = lt[g]

    shape3 = (8, 8, 32)
    grp = lax.broadcasted_iota(jnp.int32, shape3, 0)
    rowq = lax.broadcasted_iota(jnp.int32, shape3, 1) % 4
    pix = lax.broadcasted_iota(jnp.int32, shape3, 2)
    chosen = pix == rowq * 8 + grp
    low = lax.broadcasted_iota(jnp.int32, (8, HALF), 0) < 4
    targets = []
    decs = []
    for i in range(3):
        t = jnp.where(chosen, jnp.broadcast_to(tgt_ref[i][None], shape3), 0.0)
        targets.append(jnp.sum(t, axis=2, keepdims=True))
        decs.append(
            jnp.where(
                low,
                jnp.broadcast_to(dec_ref[i, :, 0:HALF], (8, HALF)),
                jnp.broadcast_to(dec_ref[i, :, HALF:FEAT], (8, HALF)),
            )[None]
        )

    def both_halves(v):
        v = jnp.broadcast_to(jnp.sum(v, axis=2, keepdims=True), (8, 8, R))
        return v + pltpu.roll(v, 4, 1)

    def wide(v):
        return jnp.concatenate([v, v], axis=2)

    def wait_l(e, c):
        l_copy(e, (g + e) % G).wait_recv()
        return c

    lax.fori_loop(1, G, wait_l, 0)
    mean = lr[...] * 0.25
    inverse = wide(lax.rsqrt(both_halves(mean * mean) * (1.0 / FEAT) + FLOOR))
    normed = mean * inverse
    normed_grad = jnp.zeros((8, 8, HALF), F32)
    square = jnp.zeros((8, 8, R), F32)
    dec_rows = []
    for i in range(3):
        residue = both_halves(normed * decs[i]) - targets[i]
        square = square + residue * residue
        res_wide = wide(residue)
        normed_grad = normed_grad + decs[i] * res_wide
        part = jnp.sum(res_wide * normed, axis=0)
        dec_rows.append(jnp.sum(part[0:4], axis=0, keepdims=True))
        dec_rows.append(jnp.sum(part[4:8], axis=0, keepdims=True))
    along = wide(both_halves(normed_grad * normed)) * (1.0 / FEAT)
    pixel_grad = inverse * (normed_grad - normed * along) * 0.25
    lb[...] = pixel_grad.astype(BF16).astype(F32)

    def b_copy(e, src):
        to = (g + e) % G
        return rc(lb.at[to], br.at[src], s_b.at[to], r_b.at[src], me, chip_of(st, to) * 2 + h)

    def send_b(e, c):
        b_copy(e, g).start()
        return c

    lax.fori_loop(1, G, send_b, 0)
    br[g] = lb[g]

    err_row = jnp.sum(jnp.sum(square, axis=0), axis=0, keepdims=True) * 0.5
    dec_rows.append(jnp.concatenate([err_row, err_row], axis=1))
    dec_rows.append(jnp.zeros((1, HALF), F32))
    decall[me] = jnp.concatenate(dec_rows, axis=0)

    def wait_b(e, c):
        b_copy(e, (g + e) % G).wait_recv()
        return c

    lax.fori_loop(1, G, wait_b, 0)
    gbuf[me, h, st] = br[...].reshape(R // 2, HALF).astype(BF16)

    def g_copy(off, k):
        ref = gbuf.at[k, h, st]
        return rc(ref, ref, s_g.at[off], r_g.at[k], depth_peer(off), lat)

    def n_copy(d, s):
        ref = gbuf.at[d, h, s]
        return rc(ref, ref, s_n.at[d], r_n.at[d], me, near)

    def pb_copy(d, half):
        return rc(gbuf.at[d, half], gbuf.at[d, half], s_pb.at[d], r_pb.at[d], me, sib)

    def d_copy(off, k):
        return rc(decall.at[k], decall.at[k], s_d.at[off], r_d.at[k], depth_peer(off), lat)

    def send_g(i, c):
        g_copy(near_offset_of(i) % K, me).start()
        return c

    lax.fori_loop(1, K, send_g, 0)

    def send_d(off, c):
        d_copy(off, me).start()
        return c

    lax.fori_loop(1, K, send_d, 0)

    def take_share(i):
        d = depth_peer(near_offset_of(i))

        @pl.when(i > 0)
        def _():
            g_copy(near_offset_of(i) % K, d).wait_recv()

        n_copy(d, st).start()

    def pass_share(i):
        d = depth_peer(near_offset_of(i))
        n_copy(d, 1 - st).wait_recv()
        pb_copy(d, h).start()

    def back_share(i):
        d = depth_peer(near_offset_of(i))
        pb_copy(d, 1 - h).wait_recv()
        grads = gbuf[d].reshape(2 * R, HALF)
        ray_grad = mm(grads, oh[d], TN)
        terms = jnp.sum(scaled[d].astype(F32) * ray_grad, axis=0, keepdims=True)
        tmall[me, pl.ds(d, 1), :] = terms[:, 0:R] + terms[:, R : 2 * R]
        sc = scl[pl.ds(d, 1), :]
        bld[d] = ray_grad * jnp.concatenate([sc, sc], axis=1)
        weight_grad = [jnp.zeros((8, R), F32) for _ in range(S)]
        for f0 in range(0, FEAT, 64):
            fh = f0 // HALF
            fg = bld[d, f0 - fh * HALF : f0 - fh * HALF + 64, fh * R : (fh + 1) * R]
            for s in range(S):
                part = feats[d, f0 : f0 + 64, s * R : (s + 1) * R].astype(F32) * fg
                weight_grad[s] = weight_grad[s] + jnp.sum(part.reshape(8, 8, R), axis=0)
                feats[d, f0 : f0 + 64, s * R : (s + 1) * R] = (
                    fg * wts[d, s : s + 1, :]
                ).astype(BF16)
        wgs[d] = jnp.concatenate(
            [jnp.sum(weight_grad[s], axis=0, keepdims=True) for s in range(S)], axis=0
        )

    def third_share(i):
        d = depth_peer(near_offset_of(i))
        g3_ref[...] += mm(h2s[d], feats[d], NT)
        b2p[d] = mm(w3_ref[...], feats[d], NN)

    g3_ref[...] = jnp.zeros_like(g3_ref)

    def back_step(i, c):
        @pl.when(i >= LATE + 1)
        def _():
            third_share(i - 1 - LATE)

        take_share(i)

        @pl.when(i >= 1)
        def _():
            pass_share(i - 1)

        @pl.when(i >= 2)
        def _():
            back_share(i - 2)

        return c

    lax.fori_loop(0, K, back_step, 0)
    third_share(K - 1 - LATE)
    pass_share(K - 1)
    back_share(K - 2)
    back_share(K - 1)

    def t_copy(off, k):
        return rc(tmall.at[k], tmall.at[k], s_t.at[off], r_t.at[k], depth_peer(off), lat)

    def send_t(off, c):
        t_copy(off, me).start()
        return c

    lax.fori_loop(1, K, send_t, 0)

    def wait_d(off, c):
        d_copy(off, depth_peer(off)).wait_recv()
        return c

    lax.fori_loop(1, K, wait_d, 0)
    dec_sum = decall[0]
    for k in range(1, K):
        dec_sum = dec_sum + decall[k]
    for i in range(3):
        gdec_ref[i, :, 0:HALF] = dec_sum[2 * i : 2 * i + 1]
        gdec_ref[i, :, HALF:FEAT] = dec_sum[2 * i + 1 : 2 * i + 2]
    esend[...] = jnp.broadcast_to(dec_sum[6:7, 0:R], (8, R))
    elat[m] = esend[...]

    def e_copy(e, src):
        to = (m + e) % CHIPS
        return rc(esend, elat.at[src], s_e.at[to], r_e.at[src], me, to * 2 + h)

    def send_e(e, c):
        e_copy(e, m).start()
        return c

    lax.fori_loop(1, CHIPS, send_e, 0)

    def third_step(i, c):
        third_share(i)
        return c

    lax.fori_loop(K - LATE, K, third_step, 0)

    def wait_t(off, c):
        t_copy(off, depth_peer(off)).wait_recv()
        return c

    lax.fori_loop(1, K, wait_t, 0)
    behind = jnp.zeros((K, R), F32)
    for k in range(K):
        behind = behind + tmall[k] * jnp.where(places[k] > mine, 1.0, 0.0)
    sub2 = lax.broadcasted_iota(jnp.int32, (S, R), 0)
    for d in range(K):
        wg = wgs[d]
        own = wg * wts[d]
        suffix = own
        for sh in (1, 2, 4):
            suffix = suffix + jnp.where(sub2 < S - sh, pltpu.roll(suffix, S - sh, 0), 0.0)
        density_grad = STEP * (wg * expi[d] - (suffix - own) - behind[d : d + 1, :])
        lg = lgs[d]
        sig = 1.0 / (1.0 + jnp.exp(-lg))
        lgrad[d] = (density_grad * sig).astype(BF16).astype(F32)

    def wait_e(e, c):
        e_copy(e, (m + e) % CHIPS).wait_recv()
        return c

    lax.fori_loop(1, CHIPS, wait_e, 0)
    err_sum = elat[0]
    for k in range(1, CHIPS):
        err_sum = err_sum + elat[k]
    epsend[...] = err_sum
    ep_copy = rc(epsend, eprec, s_ep, r_ep, me, sib)
    ep_copy.start()

    g1_ref[...] = jnp.zeros_like(g1_ref)
    g2_ref[...] = jnp.zeros_like(g2_ref)

    def last_step(d, gdens):
        lg = lgrad[d]
        lg8 = jnp.concatenate(
            [jnp.broadcast_to(lg[s : s + 1, :], (8, R)) for s in range(S)], axis=1
        )
        gdens = gdens + mm(lg8.astype(BF16), h2s[d], NT)
        for s in range(S):
            cols = slice(s * R, (s + 1) * R)
            v = b2p[d, :, cols] + wdb[...] * lg[s : s + 1, :]
            b2s[:, cols] = jnp.where(h2s[d, :, cols].astype(F32) > 0.0, v, 0.0).astype(BF16)
        g2_ref[...] += mm(h1s[d], b2s[...], NT)
        b1 = mm(w2_ref[...], b2s[...], NN)
        b1 = jnp.where(h1s[d].astype(F32) > 0.0, b1, 0.0).astype(BF16)
        g1_ref[...] += mm(take_x(d), b1, NT)
        return gdens

    gdens = lax.fori_loop(0, K, last_step, jnp.zeros((8, HID), F32))
    gd_ref[...] = gdens[0:1]

    ep_copy.wait_recv()
    err_ref[...] = (epsend[0:1, 0:1] + eprec[0:1, 0:1]) * (1.0 / COUNT)

    def end_depth(off, c):
        d = depth_peer(off)
        ds_copy(off, me).wait_send()
        z_copy(d, me).wait_send()
        g_copy(off, me).wait_send()
        d_copy(off, me).wait_send()
        t_copy(off, me).wait_send()
        l_copy(off, g).wait_send()
        b_copy(off, g).wait_send()
        return c

    lax.fori_loop(1, K, end_depth, 0)

    def end_lateral(e, c):
        e_copy(e, m).wait_send()
        return c

    lax.fori_loop(1, CHIPS, end_lateral, 0)

    def end_pair(d, c):
        pf_copy(d).wait_send()
        y_copy(d).wait_send()
        n_copy(d, st).wait_send()
        pb_copy(d, h).wait_send()
        return c

    lax.fori_loop(0, K, end_pair, 0)
    ep_copy.wait_send()


def put_out(*refs):
    for i in range(6):
        refs[6 + i][...] = refs[i][...]


def body(samples, w_first, w_second, w_third, w_density, decoder, depth_order, ray_slot, target):
    vmem = pl.BlockSpec(memory_space=pltpu.VMEM)
    dma = pltpu.SemaphoreType.DMA
    v = pltpu.VMEM
    results = ((ENC, HID), (HID, HID), (HID, FEAT), (1, HID), (3, 1, FEAT), (1, 1))
    outs = pl.pallas_call(
        kernel,
        name="step",
        out_shape=tuple(pltpu.VMEM(shape, F32) for shape in results),
        in_specs=[vmem] * 6 + [pl.BlockSpec(memory_space=pltpu.SMEM)] + [vmem] * 2,
        out_specs=(vmem,) * 6,
        scratch_shapes=[
            v((HID, ENC), BF16),
            v((HID, HID), BF16),
            v((FEAT, HID), BF16),
            v((HID, R), F32),
            v((K, HID, W), BF16),
            v((K, HID, W), BF16),
            v((K, FEAT, W), BF16),
            v((K, S, R), F32),
            v((K, S, R), F32),
            v((K, S, R), F32),
            v((K, HALF, 2 * R), F32),
            v((K, R), F32),
            v((K, HALF, 2 * R), BF16),
            v((K, 2 * R, 2 * R), BF16),
            v((K, 2, 2, R // 2, HALF), BF16),
            v((K, 2, R // 2, HALF), BF16),
            v((K, R // 2, HALF), BF16),
            v((K, R // 2, HALF), BF16),
            v((K, R // 2, HALF), BF16),
            v((K, R // 2, HALF), BF16),
            v((G, 8, HALF), F32),
            v((G, 8, HALF), F32),
            v((G, 8, HALF), F32),
            v((G, 8, HALF), F32),
            v((K, 2, 2, R // 2, HALF), BF16),
            v((K, K, R), F32),
            v((K, K, R), F32),
            v((K, S, R), F32),
            v((K, S, R), F32),
            v((HID, W), BF16),
            v((K, HID, W), F32),
            v((K, 8, HALF), F32),
            v((8, R), F32),
            v((CHIPS, 8, R), F32),
            v((8, R), F32),
            v((8, R), F32),
            dma((K,)), dma((K,)),
            dma((K,)), dma((K,)),
            dma((K,)), dma((K,)),
            dma((K,)), dma((K,)),
            dma((G,)), dma((G,)),
            dma((G,)), dma((G,)),
            dma((K,)), dma((K,)),
            dma((K,)), dma((K,)),
            dma((K,)), dma((K,)),
            dma((K,)), dma((K,)),
            dma((K,)), dma((K,)),
            dma((CHIPS,)), dma((CHIPS,)),
            dma(()), dma(()),
        ],
        compiler_params=pltpu.CompilerParams(
            collective_id=0, has_side_effects=True, vmem_limit_bytes=58 * 1024 * 1024
        ),
    )(
        samples[0, 0],
        w_first[0, 0],
        w_second[0, 0],
        w_third[0, 0],
        w_density[0],
        jnp.transpose(decoder, (1, 0, 2)),
        depth_order,
        ray_slot,
        jnp.transpose(target, (1, 0, 2)),
    )
    outs = pl.pallas_call(
        put_out,
        name="put_out",
        out_shape=tuple(jax.ShapeDtypeStruct(shape, F32) for shape in results),
        in_specs=[vmem] * 6,
        out_specs=(vmem,) * 6,
    )(*[pltpu.with_memory_space_constraint(o, pltpu.VMEM) for o in outs])
    return (
        outs[0][None, None],
        outs[1][None, None],
        outs[2][None, None],
        outs[3][None],
        jnp.transpose(outs[4], (1, 0, 2)),
        outs[5][0, 0],
    )


def solution(mesh):
    placed = (
        P("depth", "lateral", None, None),
        P("depth", "lateral", None, None),
        P("depth", "lateral", None, None),
        P("depth", "lateral", None, None),
        P("depth", "lateral", None),
        P("lateral", None, None),
        P("lateral", None),
        P("lateral", None),
        P("lateral", None, "depth"),
    )
    return jax.shard_map(
        body,
        mesh=mesh,
        in_specs=placed,
        out_specs=(
            P("depth", "lateral", None, None),
            P("depth", "lateral", None, None),
            P("depth", "lateral", None, None),
            P("depth", "lateral", None),
            P("lateral", None, None),
            P(),
        ),
        check_vma=False,
    )
```

```python
import jax
import jax.numpy as jnp
from jax import lax
from jax.experimental import pallas as pl
from jax.experimental.pallas import tpu as pltpu
from jax.sharding import PartitionSpec as P

MESH = pl.DeviceIdType.MESH
F32 = jnp.float32
BF16 = jnp.bfloat16

ENC, HID, FEAT = 64, 256, 512
S = 8
K = 8
R = 128
CHIPS = 16
G = 8
W = S * R
HALF = FEAT // 2
STEP = 0.04
FLOOR = 1e-05
COUNT = 24576.0
NEAR_LAG = 3
PAIR_LAG = 5

NN = (((1,), (0,)), ((), ()))
NT = (((1,), (1,)), ((), ()))
TN = (((0,), (0,)), ((), ()))


def mm(a, b, dims):
    return lax.dot_general(a, b, dims, preferred_element_type=F32)


def offset_of(i):
    return 4 + ((i + 1) // 2) * (1 - 2 * (i % 2))


def near_offset_of(i):
    return ((i + 1) // 2) * (2 * (i % 2) - 1) + 8


def kernel(
    x_ref, w1_ref, w2_ref, w3_ref, wd_ref, dec_ref, order_ref, slot_ref, tgt_ref,
    g1_ref, g2_ref, g3_ref, gd_ref, gdec_ref, err_ref,
    xs, w1t, w2t, w3t, wdb, h1s, h2s, feats, lgs, wts, expi, bld, scl, scaled, oh,
    pfull, prec, ysend, yrec, zsend, zrecv, lt, lr, lb, br, gbuf, dsall, tmall, wgs, lgrad, b2s, b2p,
    decall, esend, elat, epsend, eprec,
    s_x, s_ds, r_ds, s_pf, r_pf, s_y, r_y, s_z, r_z, s_l, r_l, s_b, r_b, s_g, r_g, s_n, r_n, s_pb, r_pb,
    s_t, r_t, s_d, r_d, s_e, r_e, s_ep, r_ep,
):
    me = lax.axis_index("depth")
    lat = lax.axis_index("lateral")
    h = lat % 2
    m = lat // 2
    sib = lat + 1 - 2 * h
    g = m // 2
    st = ((m % 4 + 1) // 2) % 2
    near = (m + 1 - 2 * (m % 2)) * 2 + h

    def chip_of(s, i):
        return (i // 2) * 4 + 2 * (i % 2) + (s + i) % 2

    def depth_peer(off):
        return (me + off) % K

    def rc(src, dst, ssem, rsem, z, l):
        return pltpu.make_async_remote_copy(
            src_ref=src, dst_ref=dst, send_sem=ssem, recv_sem=rsem,
            device_id=(z, l), device_id_type=MESH,
        )

    def x_copy(s):
        cols = pl.ds(pl.multiple_of(s * (K * R), K * R), K * R)
        return pltpu.make_async_copy(x_ref.at[:, cols], xs.at[s], s_x.at[s])

    for s in range(S):
        x_copy(s).start()

    barrier = pltpu.get_barrier_semaphore()

    def greet_depth(e, c):
        pl.semaphore_signal(barrier, inc=1, device_id=((me + e) % K, lat), device_id_type=MESH)
        return c

    def greet_lateral(e, c):
        pl.semaphore_signal(
            barrier, inc=1, device_id=(me, ((m + e) % CHIPS) * 2 + h), device_id_type=MESH
        )
        return c

    lax.fori_loop(1, K, greet_depth, 0)
    lax.fori_loop(1, CHIPS, greet_lateral, 0)
    pl.semaphore_signal(barrier, inc=1, device_id=(me, sib), device_id_type=MESH)

    w1t[...] = w1_ref[...].T
    w2t[...] = w2_ref[...].T
    wd8 = jnp.broadcast_to(wd_ref[...], (8, HID))
    wdb[...] = jnp.broadcast_to(wd_ref[...].astype(F32), (R, HID)).T

    def take_x(d):
        return jnp.concatenate(
            [xs[s, :, pl.ds(pl.multiple_of(d * R, R), R)] for s in range(S)], axis=1
        )

    def first_pass(s, c):
        x_copy(s).wait()
        cols = pl.ds(pl.multiple_of(s * R, R), R)
        h1 = jnp.maximum(mm(w1t[...], xs[s], NN), 0.0).astype(BF16)
        h2 = jnp.maximum(mm(w2t[...], h1, NN), 0.0).astype(BF16)
        lg = mm(wd8, h2, NN)
        for d in range(K):
            here = slice(d * R, (d + 1) * R)
            h1s[d, :, cols] = h1[:, here]
            h2s[d, :, cols] = h2[:, here]
            lgs[d, pl.ds(s, 1), :] = lg[0:1, here]
        return c

    lax.fori_loop(0, S, first_pass, 0)

    sub = lax.broadcasted_iota(jnp.int32, (K, S, R), 1)
    logits = lgs[...]
    density = jnp.maximum(logits, 0.0) + jnp.log1p(jnp.exp(-jnp.abs(logits)))
    inc = density
    for sh in (1, 2, 4):
        inc = inc + jnp.where(sub >= sh, pltpu.roll(inc, sh, 1), 0.0)
    wts[...] = jnp.exp(-STEP * (inc - density)) * (1.0 - jnp.exp(-STEP * density))
    expi[...] = jnp.exp(-STEP * inc)
    dsall[me] = STEP * jnp.concatenate([inc[d, S - 1 : S, :] for d in range(K)], axis=0)

    pl.semaphore_wait(barrier, K - 1 + CHIPS - 1 + 1)

    def ds_copy(off, k):
        return rc(dsall.at[k], dsall.at[k], s_ds.at[off], r_ds.at[k], depth_peer(off), lat)

    def send_ds(off, c):
        ds_copy(off, me).start()
        return c

    lax.fori_loop(1, K, send_ds, 0)
    w3t[...] = w3_ref[...].T

    row = lax.broadcasted_iota(jnp.int32, (2 * R, R), 0)
    code = (chip_of((row // 64) % 2, (row // 8) % G) * 2 + row // R) * 4 + row % 4
    code_lo = jnp.where((row // 4) % 2 == 0, code, -1)
    code_hi = jnp.where((row // 4) % 2 == 1, code, -1)

    def one_hot(d, c):
        slots = slot_ref[:, pl.ds(pl.multiple_of(d * R, R), R)]
        oh[d] = jnp.concatenate(
            [
                jnp.where(code_lo == slots, 1.0, 0.0).astype(BF16),
                jnp.where(code_hi == slots, 1.0, 0.0).astype(BF16),
            ],
            axis=1,
        )
        return c

    lax.fori_loop(0, K, one_hot, 0)

    def second_pass(d, c):
        feats[d] = mm(w3t[...], h2s[d], NN).astype(BF16)
        for f0 in range(0, FEAT, 64):
            total = jnp.zeros((64, R), F32)
            for s in range(S):
                total = total + feats[d, f0 : f0 + 64, s * R : (s + 1) * R].astype(F32) * wts[
                    d, s : s + 1, :
                ]
            fh = f0 // HALF
            bld[d, f0 - fh * HALF : f0 - fh * HALF + 64, fh * R : (fh + 1) * R] = total
        return c

    lax.fori_loop(0, K, second_pass, 0)

    places = []
    mine = jnp.int32(0)
    for k in range(K):
        place = jnp.int32(0)
        for p in range(K):
            place = place + jnp.where(order_ref[0, p] == k, p, 0)
        places.append(place)
    for p in range(K):
        mine = mine + jnp.where(order_ref[0, p] == me, p, 0)

    def wait_ds(off, c):
        ds_copy(off, depth_peer(off)).wait_recv()
        return c

    lax.fori_loop(1, K, wait_ds, 0)
    before = jnp.zeros((K, R), F32)
    for k in range(K):
        before = before + dsall[k] * jnp.where(places[k] < mine, 1.0, 0.0)
    scl[...] = jnp.exp(-before)

    def pf_copy(d):
        return rc(pfull.at[d, 1 - h], prec.at[d], s_pf.at[d], r_pf.at[d], me, sib)

    def y_copy(d):
        return rc(ysend.at[d], yrec.at[d], s_y.at[d], r_y.at[d], me, near)

    def z_copy(d, k):
        return rc(zsend.at[d], zrecv.at[k], s_z.at[d], r_z.at[k], d, lat)

    def make_scaled(i, c):
        d = depth_peer(offset_of(i))
        sc = scl[pl.ds(d, 1), :]
        sc = jnp.concatenate([sc, sc], axis=1)
        scaled[d] = (bld[d] * sc).astype(BF16)
        placed = mm(oh[d], scaled[d], NT).astype(BF16)
        for half in range(2):
            for s in range(2):
                r0 = half * R + s * 64
                pfull[d, half, s] = placed[r0 : r0 + 64]
        pf_copy(d).start()
        return c

    lax.fori_loop(0, K, make_scaled, 0)

    def pair_sum(d, s):
        return pfull[d, h, s].astype(F32) + prec[d, s].astype(F32)

    def send_near(i, c):
        d = depth_peer(offset_of(i))
        pf_copy(d).wait_recv()
        ysend[d] = pair_sum(d, 1 - st).astype(BF16)
        y_copy(d).start()
        return c

    lax.fori_loop(0, K, send_near, 0)

    def group_sum(d):
        y_copy(d).wait_recv()
        return (pair_sum(d, st) + yrec[d].astype(F32)).astype(BF16)

    def send_share(i, c):
        d = depth_peer(offset_of(i))
        zsend[d] = group_sum(d)
        z_copy(d, me).start()
        return c

    lax.fori_loop(0, K - 1, send_share, 0)
    zrecv[me] = group_sum(me)

    def wait_z(off, c):
        z_copy(me, depth_peer(off)).wait_recv()
        return c

    lax.fori_loop(1, K, wait_z, 0)
    total = zrecv[0].astype(F32)
    for k in range(1, K):
        total = total + zrecv[k].astype(F32)
    lt[...] = total.reshape(G, 8, HALF)

    def l_copy(e, src):
        to = (g + e) % G
        return rc(lt.at[to], lr.at[src], s_l.at[to], r_l.at[src], me, chip_of(st, to) * 2 + h)

    def send_l(e, c):
        l_copy(e, g).start()
        return c

    lax.fori_loop(1, G, send_l, 0)
    lr[g] = lt[g]

    shape3 = (8, 8, 32)
    grp = lax.broadcasted_iota(jnp.int32, shape3, 0)
    rowq = lax.broadcasted_iota(jnp.int32, shape3, 1) % 4
    pix = lax.broadcasted_iota(jnp.int32, shape3, 2)
    chosen = pix == rowq * 8 + grp
    low = lax.broadcasted_iota(jnp.int32, (8, HALF), 0) < 4
    targets = []
    decs = []
    for i in range(3):
        t = jnp.where(chosen, jnp.broadcast_to(tgt_ref[i][None], shape3), 0.0)
        targets.append(jnp.sum(t, axis=2, keepdims=True))
        decs.append(
            jnp.where(
                low,
                jnp.broadcast_to(dec_ref[i, :, 0:HALF], (8, HALF)),
                jnp.broadcast_to(dec_ref[i, :, HALF:FEAT], (8, HALF)),
            )[None]
        )

    def both_halves(v):
        v = jnp.broadcast_to(jnp.sum(v, axis=2, keepdims=True), (8, 8, R))
        return v + pltpu.roll(v, 4, 1)

    def wide(v):
        return jnp.concatenate([v, v], axis=2)

    def wait_l(e, c):
        l_copy(e, (g + e) % G).wait_recv()
        return c

    lax.fori_loop(1, G, wait_l, 0)
    mean = lr[...] * 0.25
    inverse = wide(lax.rsqrt(both_halves(mean * mean) * (1.0 / FEAT) + FLOOR))
    normed = mean * inverse
    normed_grad = jnp.zeros((8, 8, HALF), F32)
    square = jnp.zeros((8, 8, R), F32)
    dec_rows = []
    for i in range(3):
        residue = both_halves(normed * decs[i]) - targets[i]
        square = square + residue * residue
        res_wide = wide(residue)
        normed_grad = normed_grad + decs[i] * res_wide
        part = jnp.sum(res_wide * normed, axis=0)
        dec_rows.append(jnp.sum(part[0:4], axis=0, keepdims=True))
        dec_rows.append(jnp.sum(part[4:8], axis=0, keepdims=True))
    along = wide(both_halves(normed_grad * normed)) * (1.0 / FEAT)
    pixel_grad = inverse * (normed_grad - normed * along) * 0.25
    lb[...] = pixel_grad.astype(BF16).astype(F32)

    def b_copy(e, src):
        to = (g + e) % G
        return rc(lb.at[to], br.at[src], s_b.at[to], r_b.at[src], me, chip_of(st, to) * 2 + h)

    def send_b(e, c):
        b_copy(e, g).start()
        return c

    lax.fori_loop(1, G, send_b, 0)
    br[g] = lb[g]

    err_row = jnp.sum(jnp.sum(square, axis=0), axis=0, keepdims=True) * 0.5
    dec_rows.append(jnp.concatenate([err_row, err_row], axis=1))
    dec_rows.append(jnp.zeros((1, HALF), F32))
    decall[me] = jnp.concatenate(dec_rows, axis=0)

    def wait_b(e, c):
        b_copy(e, (g + e) % G).wait_recv()
        return c

    lax.fori_loop(1, G, wait_b, 0)
    gbuf[me, h, st] = br[...].reshape(R // 2, HALF).astype(BF16)

    def g_copy(off, k):
        ref = gbuf.at[k, h, st]
        return rc(ref, ref, s_g.at[off], r_g.at[k], depth_peer(off), lat)

    def n_copy(d, s):
        ref = gbuf.at[d, h, s]
        return rc(ref, ref, s_n.at[d], r_n.at[d], me, near)

    def pb_copy(d, half):
        return rc(gbuf.at[d, half], gbuf.at[d, half], s_pb.at[d], r_pb.at[d], me, sib)

    def d_copy(off, k):
        return rc(decall.at[k], decall.at[k], s_d.at[off], r_d.at[k], depth_peer(off), lat)

    def send_g(i, c):
        g_copy(near_offset_of(i) % K, me).start()
        return c

    lax.fori_loop(1, K, send_g, 0)

    def send_d(off, c):
        d_copy(off, me).start()
        return c

    lax.fori_loop(1, K, send_d, 0)

    def take_share(i):
        d = depth_peer(near_offset_of(i))

        @pl.when(i > 0)
        def _():
            g_copy(near_offset_of(i) % K, d).wait_recv()

        n_copy(d, st).start()

    def pass_share(i):
        d = depth_peer(near_offset_of(i))
        n_copy(d, 1 - st).wait_recv()
        pb_copy(d, h).start()

    def back_share(i):
        d = depth_peer(near_offset_of(i))
        pb_copy(d, 1 - h).wait_recv()
        grads = gbuf[d].reshape(2 * R, HALF)
        ray_grad = mm(grads, oh[d], TN)
        terms = jnp.sum(scaled[d].astype(F32) * ray_grad, axis=0, keepdims=True)
        tmall[me, pl.ds(d, 1), :] = terms[:, 0:R] + terms[:, R : 2 * R]
        sc = scl[pl.ds(d, 1), :]
        bld[d] = ray_grad * jnp.concatenate([sc, sc], axis=1)
        weight_grad = [jnp.zeros((8, R), F32) for _ in range(S)]
        for f0 in range(0, FEAT, 64):
            fh = f0 // HALF
            fg = bld[d, f0 - fh * HALF : f0 - fh * HALF + 64, fh * R : (fh + 1) * R]
            for s in range(S):
                part = feats[d, f0 : f0 + 64, s * R : (s + 1) * R].astype(F32) * fg
                weight_grad[s] = weight_grad[s] + jnp.sum(part.reshape(8, 8, R), axis=0)
                feats[d, f0 : f0 + 64, s * R : (s + 1) * R] = (
                    fg * wts[d, s : s + 1, :]
                ).astype(BF16)
        wgs[d] = jnp.concatenate(
            [jnp.sum(weight_grad[s], axis=0, keepdims=True) for s in range(S)], axis=0
        )

    def back_step(i, c):
        @pl.when(i < K)
        def _():
            take_share(i)

        @pl.when((i >= NEAR_LAG) & (i < K + NEAR_LAG))
        def _():
            pass_share(i - NEAR_LAG)

        @pl.when(i >= PAIR_LAG)
        def _():
            back_share(i - PAIR_LAG)

        return c

    lax.fori_loop(0, K + PAIR_LAG, back_step, 0)

    def t_copy(off, k):
        return rc(tmall.at[k], tmall.at[k], s_t.at[off], r_t.at[k], depth_peer(off), lat)

    def send_t(off, c):
        t_copy(off, me).start()
        return c

    lax.fori_loop(1, K, send_t, 0)

    def wait_d(off, c):
        d_copy(off, depth_peer(off)).wait_recv()
        return c

    lax.fori_loop(1, K, wait_d, 0)
    dec_sum = decall[0]
    for k in range(1, K):
        dec_sum = dec_sum + decall[k]
    for i in range(3):
        gdec_ref[i, :, 0:HALF] = dec_sum[2 * i : 2 * i + 1]
        gdec_ref[i, :, HALF:FEAT] = dec_sum[2 * i + 1 : 2 * i + 2]
    esend[...] = jnp.broadcast_to(dec_sum[6:7, 0:R], (8, R))
    elat[m] = esend[...]

    def e_copy(e, src):
        to = (m + e) % CHIPS
        return rc(esend, elat.at[src], s_e.at[to], r_e.at[src], me, to * 2 + h)

    def send_e(e, c):
        e_copy(e, m).start()
        return c

    lax.fori_loop(1, CHIPS, send_e, 0)

    g3_ref[...] = jnp.zeros_like(g3_ref)

    def third_step(d, c):
        g3_ref[...] += mm(h2s[d], feats[d], NT)
        b2p[d] = mm(w3_ref[...], feats[d], NN)
        return c

    lax.fori_loop(0, K, third_step, 0)

    def wait_t(off, c):
        t_copy(off, depth_peer(off)).wait_recv()
        return c

    lax.fori_loop(1, K, wait_t, 0)
    behind = jnp.zeros((K, R), F32)
    for k in range(K):
        behind = behind + tmall[k] * jnp.where(places[k] > mine, 1.0, 0.0)
    sub2 = lax.broadcasted_iota(jnp.int32, (S, R), 0)
    for d in range(K):
        wg = wgs[d]
        own = wg * wts[d]
        suffix = own
        for sh in (1, 2, 4):
            suffix = suffix + jnp.where(sub2 < S - sh, pltpu.roll(suffix, S - sh, 0), 0.0)
        density_grad = STEP * (wg * expi[d] - (suffix - own) - behind[d : d + 1, :])
        lg = lgs[d]
        sig = 1.0 / (1.0 + jnp.exp(-lg))
        lgrad[d] = (density_grad * sig).astype(BF16).astype(F32)

    def wait_e(e, c):
        e_copy(e, (m + e) % CHIPS).wait_recv()
        return c

    lax.fori_loop(1, CHIPS, wait_e, 0)
    err_sum = elat[0]
    for k in range(1, CHIPS):
        err_sum = err_sum + elat[k]
    epsend[...] = err_sum
    ep_copy = rc(epsend, eprec, s_ep, r_ep, me, sib)
    ep_copy.start()

    g1_ref[...] = jnp.zeros_like(g1_ref)
    g2_ref[...] = jnp.zeros_like(g2_ref)

    def last_step(d, gdens):
        lg = lgrad[d]
        lg8 = jnp.concatenate(
            [jnp.broadcast_to(lg[s : s + 1, :], (8, R)) for s in range(S)], axis=1
        )
        gdens = gdens + mm(lg8.astype(BF16), h2s[d], NT)
        for s in range(S):
            cols = slice(s * R, (s + 1) * R)
            v = b2p[d, :, cols] + wdb[...] * lg[s : s + 1, :]
            b2s[:, cols] = jnp.where(h2s[d, :, cols].astype(F32) > 0.0, v, 0.0).astype(BF16)
        g2_ref[...] += mm(h1s[d], b2s[...], NT)
        b1 = mm(w2_ref[...], b2s[...], NN)
        b1 = jnp.where(h1s[d].astype(F32) > 0.0, b1, 0.0).astype(BF16)
        g1_ref[...] += mm(take_x(d), b1, NT)
        return gdens

    gdens = lax.fori_loop(0, K, last_step, jnp.zeros((8, HID), F32))
    gd_ref[...] = gdens[0:1]

    ep_copy.wait_recv()
    err_ref[...] = (epsend[0:1, 0:1] + eprec[0:1, 0:1]) * (1.0 / COUNT)

    def end_depth(off, c):
        d = depth_peer(off)
        ds_copy(off, me).wait_send()
        z_copy(d, me).wait_send()
        g_copy(off, me).wait_send()
        d_copy(off, me).wait_send()
        t_copy(off, me).wait_send()
        l_copy(off, g).wait_send()
        b_copy(off, g).wait_send()
        return c

    lax.fori_loop(1, K, end_depth, 0)

    def end_lateral(e, c):
        e_copy(e, m).wait_send()
        return c

    lax.fori_loop(1, CHIPS, end_lateral, 0)

    def end_pair(d, c):
        pf_copy(d).wait_send()
        y_copy(d).wait_send()
        n_copy(d, st).wait_send()
        pb_copy(d, h).wait_send()
        return c

    lax.fori_loop(0, K, end_pair, 0)
    ep_copy.wait_send()


def put_out(*refs):
    for i in range(6):
        refs[6 + i][...] = refs[i][...]


def body(samples, w_first, w_second, w_third, w_density, decoder, depth_order, ray_slot, target):
    vmem = pl.BlockSpec(memory_space=pltpu.VMEM)
    dma = pltpu.SemaphoreType.DMA
    v = pltpu.VMEM
    results = ((ENC, HID), (HID, HID), (HID, FEAT), (1, HID), (3, 1, FEAT), (1, 1))
    outs = pl.pallas_call(
        kernel,
        name="step",
        out_shape=tuple(pltpu.VMEM(shape, F32) for shape in results),
        in_specs=[pl.BlockSpec(memory_space=pl.ANY)] + [vmem] * 5 + [pl.BlockSpec(memory_space=pltpu.SMEM)] + [vmem] * 2,
        out_specs=(vmem,) * 6,
        scratch_shapes=[
            v((S, ENC, K * R), BF16),
            v((HID, ENC), BF16),
            v((HID, HID), BF16),
            v((FEAT, HID), BF16),
            v((HID, R), F32),
            v((K, HID, W), BF16),
            v((K, HID, W), BF16),
            v((K, FEAT, W), BF16),
            v((K, S, R), F32),
            v((K, S, R), F32),
            v((K, S, R), F32),
            v((K, HALF, 2 * R), F32),
            v((K, R), F32),
            v((K, HALF, 2 * R), BF16),
            v((K, 2 * R, 2 * R), BF16),
            v((K, 2, 2, R // 2, HALF), BF16),
            v((K, 2, R // 2, HALF), BF16),
            v((K, R // 2, HALF), BF16),
            v((K, R // 2, HALF), BF16),
            v((K, R // 2, HALF), BF16),
            v((K, R // 2, HALF), BF16),
            v((G, 8, HALF), F32),
            v((G, 8, HALF), F32),
            v((G, 8, HALF), F32),
            v((G, 8, HALF), F32),
            v((K, 2, 2, R // 2, HALF), BF16),
            v((K, K, R), F32),
            v((K, K, R), F32),
            v((K, S, R), F32),
            v((K, S, R), F32),
            v((HID, W), BF16),
            v((K, HID, W), F32),
            v((K, 8, HALF), F32),
            v((8, R), F32),
            v((CHIPS, 8, R), F32),
            v((8, R), F32),
            v((8, R), F32),
            dma((S,)),
            dma((K,)), dma((K,)),
            dma((K,)), dma((K,)),
            dma((K,)), dma((K,)),
            dma((K,)), dma((K,)),
            dma((G,)), dma((G,)),
            dma((G,)), dma((G,)),
            dma((K,)), dma((K,)),
            dma((K,)), dma((K,)),
            dma((K,)), dma((K,)),
            dma((K,)), dma((K,)),
            dma((K,)), dma((K,)),
            dma((CHIPS,)), dma((CHIPS,)),
            dma(()), dma(()),
        ],
        compiler_params=pltpu.CompilerParams(
            collective_id=0, has_side_effects=True, vmem_limit_bytes=58 * 1024 * 1024
        ),
    )(
        samples[0, 0],
        w_first[0, 0],
        w_second[0, 0],
        w_third[0, 0],
        w_density[0],
        jnp.transpose(decoder, (1, 0, 2)),
        depth_order,
        ray_slot,
        jnp.transpose(target, (1, 0, 2)),
    )
    outs = pl.pallas_call(
        put_out,
        name="put_out",
        out_shape=tuple(jax.ShapeDtypeStruct(shape, F32) for shape in results),
        in_specs=[vmem] * 6,
        out_specs=(vmem,) * 6,
    )(*[pltpu.with_memory_space_constraint(o, pltpu.VMEM) for o in outs])
    return (
        outs[0][None, None],
        outs[1][None, None],
        outs[2][None, None],
        outs[3][None],
        jnp.transpose(outs[4], (1, 0, 2)),
        outs[5][0, 0],
    )


def solution(mesh):
    placed = (
        P("depth", "lateral", None, None),
        P("depth", "lateral", None, None),
        P("depth", "lateral", None, None),
        P("depth", "lateral", None, None),
        P("depth", "lateral", None),
        P("lateral", None, None),
        P("lateral", None),
        P("lateral", None),
        P("lateral", None, "depth"),
    )
    return jax.shard_map(
        body,
        mesh=mesh,
        in_specs=placed,
        out_specs=(
            P("depth", "lateral", None, None),
            P("depth", "lateral", None, None),
            P("depth", "lateral", None, None),
            P("depth", "lateral", None),
            P("lateral", None, None),
            P(),
        ),
        check_vma=False,
    )
```

```python
import jax
import jax.numpy as jnp
from jax import lax
from jax.experimental import pallas as pl
from jax.experimental.pallas import tpu as pltpu
from jax.sharding import PartitionSpec as P

MESH = pl.DeviceIdType.MESH
F32 = jnp.float32
BF16 = jnp.bfloat16

ENC, HID, FEAT = 64, 256, 512
S = 8
K = 8
R = 128
CHIPS = 16
G = 8
W = S * R
HALF = FEAT // 2
STEP = 0.04
FLOOR = 1e-05
COUNT = 24576.0
NEAR_LAG = 4
PAIR_LAG = 7
FIRST = 3

NN = (((1,), (0,)), ((), ()))
NT = (((1,), (1,)), ((), ()))
TN = (((0,), (0,)), ((), ()))


def mm(a, b, dims):
    return lax.dot_general(a, b, dims, preferred_element_type=F32)


def offset_of(i):
    return 4 + ((i + 1) // 2) * (1 - 2 * (i % 2))


def near_offset_of(i):
    return ((i + 1) // 2) * (2 * (i % 2) - 1) + 8


def kernel(
    x_ref, w1_ref, w2_ref, w3_ref, wd_ref, dec_ref, order_ref, slot_ref, tgt_ref,
    g1_ref, g2_ref, g3_ref, gd_ref, gdec_ref, err_ref,
    xs, w1t, w2t, w3t, wdb, h1s, h2s, feats, lgs, wts, expi, bld, scl, scaled, oh,
    pfull, prec, ysend, yrec, zsend, zrecv, lt, lr, lb, br, gbuf, dsall, tmall, wgs, lgrad, b2s, b2t, b2p,
    decall, esend, elat, epsend, eprec,
    s_x, s_ds, r_ds, s_pf, r_pf, s_y, r_y, s_z, r_z, s_l, r_l, s_b, r_b, s_g, r_g, s_n, r_n, s_pb, r_pb,
    s_t, r_t, s_d, r_d, s_e, r_e, s_ep, r_ep,
):
    me = lax.axis_index("depth")
    lat = lax.axis_index("lateral")
    h = lat % 2
    m = lat // 2
    sib = lat + 1 - 2 * h
    g = m // 2
    st = ((m % 4 + 1) // 2) % 2
    near = (m + 1 - 2 * (m % 2)) * 2 + h

    def chip_of(s, i):
        return (i // 2) * 4 + 2 * (i % 2) + (s + i) % 2

    def depth_peer(off):
        return (me + off) % K

    def rc(src, dst, ssem, rsem, z, l):
        return pltpu.make_async_remote_copy(
            src_ref=src, dst_ref=dst, send_sem=ssem, recv_sem=rsem,
            device_id=(z, l), device_id_type=MESH,
        )

    def x_copy(s):
        cols = pl.ds(pl.multiple_of(s * (K * R), K * R), K * R)
        return pltpu.make_async_copy(x_ref.at[:, cols], xs.at[s], s_x.at[s])

    for s in range(S):
        x_copy(s).start()

    barrier = pltpu.get_barrier_semaphore()

    def greet_depth(e, c):
        pl.semaphore_signal(barrier, inc=1, device_id=((me + e) % K, lat), device_id_type=MESH)
        return c

    def greet_lateral(e, c):
        pl.semaphore_signal(
            barrier, inc=1, device_id=(me, ((m + e) % CHIPS) * 2 + h), device_id_type=MESH
        )
        return c

    lax.fori_loop(1, K, greet_depth, 0)
    lax.fori_loop(1, CHIPS, greet_lateral, 0)
    pl.semaphore_signal(barrier, inc=1, device_id=(me, sib), device_id_type=MESH)

    w1t[...] = w1_ref[...].T
    w2t[...] = w2_ref[...].T
    wd8 = jnp.broadcast_to(wd_ref[...], (8, HID))
    wdb[...] = jnp.broadcast_to(wd_ref[...].astype(F32), (R, HID)).T

    def take_x(d):
        return jnp.concatenate(
            [xs[s, :, pl.ds(pl.multiple_of(d * R, R), R)] for s in range(S)], axis=1
        )

    def first_pass(s, c):
        x_copy(s).wait()
        cols = pl.ds(pl.multiple_of(s * R, R), R)
        h1 = jnp.maximum(mm(w1t[...], xs[s], NN).astype(BF16), 0)
        h2 = jnp.maximum(mm(w2t[...], h1, NN).astype(BF16), 0)
        lg = mm(wd8, h2, NN)
        for d in range(K):
            here = slice(d * R, (d + 1) * R)
            h1s[d, :, cols] = h1[:, here]
            h2s[d, :, cols] = h2[:, here]
            lgs[d, pl.ds(s, 1), :] = lg[0:1, here]
        return c

    lax.fori_loop(0, S, first_pass, 0)

    sub = lax.broadcasted_iota(jnp.int32, (K, S, R), 1)
    logits = lgs[...]
    density = jnp.maximum(logits, 0.0) + jnp.log1p(jnp.exp(-jnp.abs(logits)))
    inc = density
    for sh in (1, 2, 4):
        inc = inc + jnp.where(sub >= sh, pltpu.roll(inc, sh, 1), 0.0)
    wts[...] = jnp.exp(-STEP * (inc - density)) * (1.0 - jnp.exp(-STEP * density))
    expi[...] = jnp.exp(-STEP * inc)
    dsall[me] = STEP * jnp.concatenate([inc[d, S - 1 : S, :] for d in range(K)], axis=0)

    pl.semaphore_wait(barrier, K - 1 + CHIPS - 1 + 1)

    def ds_copy(off, k):
        return rc(dsall.at[k], dsall.at[k], s_ds.at[off], r_ds.at[k], depth_peer(off), lat)

    def send_ds(off, c):
        ds_copy(off, me).start()
        return c

    lax.fori_loop(1, K, send_ds, 0)
    w3t[...] = w3_ref[...].T

    row = lax.broadcasted_iota(jnp.int32, (2 * R, R), 0)
    code = (chip_of((row // 64) % 2, (row // 8) % G) * 2 + row // R) * 4 + row % 4
    code_lo = jnp.where((row // 4) % 2 == 0, code, -1)
    code_hi = jnp.where((row // 4) % 2 == 1, code, -1)

    def one_hot(d, c):
        slots = slot_ref[:, pl.ds(pl.multiple_of(d * R, R), R)]
        oh[d] = jnp.concatenate(
            [
                jnp.where(code_lo == slots, 1.0, 0.0).astype(BF16),
                jnp.where(code_hi == slots, 1.0, 0.0).astype(BF16),
            ],
            axis=1,
        )
        return c

    lax.fori_loop(0, K, one_hot, 0)

    def second_pass(d, c):
        feats[d] = mm(w3t[...], h2s[d], NN).astype(BF16)
        for f0 in range(0, FEAT, 64):
            total = jnp.zeros((64, R), F32)
            for s in range(S):
                total = total + feats[d, f0 : f0 + 64, s * R : (s + 1) * R].astype(F32) * wts[
                    d, s : s + 1, :
                ]
            fh = f0 // HALF
            bld[d, f0 - fh * HALF : f0 - fh * HALF + 64, fh * R : (fh + 1) * R] = total
        return c

    lax.fori_loop(0, K, second_pass, 0)

    places = []
    mine = jnp.int32(0)
    for k in range(K):
        place = jnp.int32(0)
        for p in range(K):
            place = place + jnp.where(order_ref[0, p] == k, p, 0)
        places.append(place)
    for p in range(K):
        mine = mine + jnp.where(order_ref[0, p] == me, p, 0)

    def wait_ds(off, c):
        ds_copy(off, depth_peer(off)).wait_recv()
        return c

    lax.fori_loop(1, K, wait_ds, 0)
    before = jnp.zeros((K, R), F32)
    for k in range(K):
        before = before + dsall[k] * jnp.where(places[k] < mine, 1.0, 0.0)
    scl[...] = jnp.exp(-before)

    def pf_copy(d):
        return rc(pfull.at[d, 1 - h], prec.at[d], s_pf.at[d], r_pf.at[d], me, sib)

    def y_copy(d):
        return rc(ysend.at[d], yrec.at[d], s_y.at[d], r_y.at[d], me, near)

    def z_copy(d, k):
        return rc(zsend.at[d], zrecv.at[k], s_z.at[d], r_z.at[k], d, lat)

    def make_scaled(i, c):
        d = depth_peer(offset_of(i))
        sc = scl[pl.ds(d, 1), :]
        sc = jnp.concatenate([sc, sc], axis=1)
        scaled[d] = (bld[d] * sc).astype(BF16)
        placed = mm(oh[d], scaled[d], NT).astype(BF16)
        for half in range(2):
            for s in range(2):
                r0 = half * R + s * 64
                pfull[d, half, s] = placed[r0 : r0 + 64]
        pf_copy(d).start()
        return c

    lax.fori_loop(0, K, make_scaled, 0)

    def pair_sum(d, s):
        return pfull[d, h, s].astype(F32) + prec[d, s].astype(F32)

    def send_near(i, c):
        d = depth_peer(offset_of(i))
        pf_copy(d).wait_recv()
        ysend[d] = pair_sum(d, 1 - st).astype(BF16)
        y_copy(d).start()
        return c

    lax.fori_loop(0, K, send_near, 0)

    def group_sum(d):
        y_copy(d).wait_recv()
        return (pair_sum(d, st) + yrec[d].astype(F32)).astype(BF16)

    def send_share(i, c):
        d = depth_peer(offset_of(i))
        zsend[d] = group_sum(d)
        z_copy(d, me).start()
        return c

    lax.fori_loop(0, K - 1, send_share, 0)
    zrecv[me] = group_sum(me)

    def wait_z(off, c):
        z_copy(me, depth_peer(off)).wait_recv()
        return c

    lax.fori_loop(1, K, wait_z, 0)
    total = zrecv[0].astype(F32)
    for k in range(1, K):
        total = total + zrecv[k].astype(F32)
    lt[...] = total.reshape(G, 8, HALF)

    def l_copy(e, src):
        to = (g + e) % G
        return rc(lt.at[to], lr.at[src], s_l.at[to], r_l.at[src], me, chip_of(st, to) * 2 + h)

    def send_l(e, c):
        l_copy(e, g).start()
        return c

    lax.fori_loop(1, G, send_l, 0)
    lr[g] = lt[g]

    shape3 = (8, 8, 32)
    grp = lax.broadcasted_iota(jnp.int32, shape3, 0)
    rowq = lax.broadcasted_iota(jnp.int32, shape3, 1) % 4
    pix = lax.broadcasted_iota(jnp.int32, shape3, 2)
    chosen = pix == rowq * 8 + grp
    low = lax.broadcasted_iota(jnp.int32, (8, HALF), 0) < 4
    targets = []
    decs = []
    for i in range(3):
        t = jnp.where(chosen, jnp.broadcast_to(tgt_ref[i][None], shape3), 0.0)
        targets.append(jnp.sum(t, axis=2, keepdims=True))
        decs.append(
            jnp.where(
                low,
                jnp.broadcast_to(dec_ref[i, :, 0:HALF], (8, HALF)),
                jnp.broadcast_to(dec_ref[i, :, HALF:FEAT], (8, HALF)),
            )[None]
        )

    def both_halves(v):
        v = jnp.broadcast_to(jnp.sum(v, axis=2, keepdims=True), (8, 8, R))
        return v + pltpu.roll(v, 4, 1)

    def wide(v):
        return jnp.concatenate([v, v], axis=2)

    def wait_l(e, c):
        l_copy(e, (g + e) % G).wait_recv()
        return c

    lax.fori_loop(1, G, wait_l, 0)
    mean = lr[...] * 0.25
    inverse = wide(lax.rsqrt(both_halves(mean * mean) * (1.0 / FEAT) + FLOOR))
    normed = mean * inverse
    normed_grad = jnp.zeros((8, 8, HALF), F32)
    square = jnp.zeros((8, 8, R), F32)
    dec_rows = []
    for i in range(3):
        residue = both_halves(normed * decs[i]) - targets[i]
        square = square + residue * residue
        res_wide = wide(residue)
        normed_grad = normed_grad + decs[i] * res_wide
        part = jnp.sum(res_wide * normed, axis=0)
        dec_rows.append(jnp.sum(part[0:4], axis=0, keepdims=True))
        dec_rows.append(jnp.sum(part[4:8], axis=0, keepdims=True))
    along = wide(both_halves(normed_grad * normed)) * (1.0 / FEAT)
    pixel_grad = inverse * (normed_grad - normed * along) * 0.25
    lb[...] = pixel_grad.astype(BF16).astype(F32)

    def b_copy(e, src):
        to = (g + e) % G
        return rc(lb.at[to], br.at[src], s_b.at[to], r_b.at[src], me, chip_of(st, to) * 2 + h)

    def send_b(e, c):
        b_copy(e, g).start()
        return c

    lax.fori_loop(1, G, send_b, 0)
    br[g] = lb[g]

    err_row = jnp.sum(jnp.sum(square, axis=0), axis=0, keepdims=True) * 0.5
    dec_rows.append(jnp.concatenate([err_row, err_row], axis=1))
    dec_rows.append(jnp.zeros((1, HALF), F32))
    decall[me] = jnp.concatenate(dec_rows, axis=0)

    def wait_b(e, c):
        b_copy(e, (g + e) % G).wait_recv()
        return c

    lax.fori_loop(1, G, wait_b, 0)
    gbuf[me, h, st] = br[...].reshape(R // 2, HALF).astype(BF16)

    def g_copy(off, k):
        ref = gbuf.at[k, h, st]
        return rc(ref, ref, s_g.at[off], r_g.at[k], depth_peer(off), lat)

    def n_copy(d, s):
        ref = gbuf.at[d, h, s]
        return rc(ref, ref, s_n.at[d], r_n.at[d], me, near)

    def pb_copy(d, half):
        return rc(gbuf.at[d, half], gbuf.at[d, half], s_pb.at[d], r_pb.at[d], me, sib)

    def d_copy(off, k):
        return rc(decall.at[k], decall.at[k], s_d.at[off], r_d.at[k], depth_peer(off), lat)

    def send_g(i, c):
        g_copy(near_offset_of(i) % K, me).start()
        return c

    lax.fori_loop(1, K, send_g, 0)

    def send_d(off, c):
        d_copy(off, me).start()
        return c

    lax.fori_loop(1, K, send_d, 0)

    def take_share(i):
        d = depth_peer(near_offset_of(i))

        @pl.when(i > 0)
        def _():
            g_copy(near_offset_of(i) % K, d).wait_recv()

        n_copy(d, st).start()

    def pass_share(i):
        d = depth_peer(near_offset_of(i))
        n_copy(d, 1 - st).wait_recv()
        pb_copy(d, h).start()

    def back_share(i):
        d = depth_peer(near_offset_of(i))
        pb_copy(d, 1 - h).wait_recv()
        grads = gbuf[d].reshape(2 * R, HALF)
        ray_grad = mm(grads, oh[d], TN)
        terms = jnp.sum(scaled[d].astype(F32) * ray_grad, axis=0, keepdims=True)
        tmall[me, pl.ds(d, 1), :] = terms[:, 0:R] + terms[:, R : 2 * R]
        sc = scl[pl.ds(d, 1), :]
        bld[d] = ray_grad * jnp.concatenate([sc, sc], axis=1)
        weight_grad = [jnp.zeros((8, R), F32) for _ in range(S)]
        for f0 in range(0, FEAT, 64):
            fh = f0 // HALF
            fg = bld[d, f0 - fh * HALF : f0 - fh * HALF + 64, fh * R : (fh + 1) * R]
            for s in range(S):
                part = feats[d, f0 : f0 + 64, s * R : (s + 1) * R].astype(F32) * fg
                weight_grad[s] = weight_grad[s] + jnp.sum(part.reshape(8, 8, R), axis=0)
                feats[d, f0 : f0 + 64, s * R : (s + 1) * R] = (
                    fg * wts[d, s : s + 1, :]
                ).astype(BF16)
        wgs[d] = jnp.concatenate(
            [jnp.sum(weight_grad[s], axis=0, keepdims=True) for s in range(S)], axis=0
        )

    def third_share(d):
        g3_ref[...] += mm(h2s[d], feats[d], NT)
        b2p[d] = mm(w3_ref[...], feats[d], NN)

    g3_ref[...] = jnp.zeros_like(g3_ref)

    def back_step(i, c):
        @pl.when((i == FIRST) | (i > PAIR_LAG))
        def _():
            back_share(jnp.where(i == FIRST, 0, i - PAIR_LAG))

        @pl.when(i == FIRST + 1)
        def _():
            third_share(me)

        @pl.when(i < K)
        def _():
            take_share(i)

        @pl.when((i == 0) | ((i > NEAR_LAG) & (i < K + NEAR_LAG)))
        def _():
            pass_share(jnp.where(i == 0, 0, i - NEAR_LAG))

        return c

    lax.fori_loop(0, K + PAIR_LAG, back_step, 0)

    def t_copy(off, k):
        return rc(tmall.at[k], tmall.at[k], s_t.at[off], r_t.at[k], depth_peer(off), lat)

    def send_t(off, c):
        t_copy(off, me).start()
        return c

    lax.fori_loop(1, K, send_t, 0)

    def wait_d(off, c):
        d_copy(off, depth_peer(off)).wait_recv()
        return c

    lax.fori_loop(1, K, wait_d, 0)
    dec_sum = decall[0]
    for k in range(1, K):
        dec_sum = dec_sum + decall[k]
    for i in range(3):
        gdec_ref[i, :, 0:HALF] = dec_sum[2 * i : 2 * i + 1]
        gdec_ref[i, :, HALF:FEAT] = dec_sum[2 * i + 1 : 2 * i + 2]
    esend[...] = jnp.broadcast_to(dec_sum[6:7, 0:R], (8, R))
    elat[m] = esend[...]

    def e_copy(e, src):
        to = (m + e) % CHIPS
        return rc(esend, elat.at[src], s_e.at[to], r_e.at[src], me, to * 2 + h)

    def send_e(e, c):
        e_copy(e, m).start()
        return c

    lax.fori_loop(1, CHIPS, send_e, 0)

    def third_step(i, c):
        third_share(depth_peer(i))
        return c

    lax.fori_loop(1, K, third_step, 0)

    def wait_t(off, c):
        t_copy(off, depth_peer(off)).wait_recv()
        return c

    lax.fori_loop(1, K, wait_t, 0)
    behind = jnp.zeros((K, R), F32)
    for k in range(K):
        behind = behind + tmall[k] * jnp.where(places[k] > mine, 1.0, 0.0)
    sub2 = lax.broadcasted_iota(jnp.int32, (S, R), 0)
    for d in range(K):
        wg = wgs[d]
        own = wg * wts[d]
        suffix = own
        for sh in (1, 2, 4):
            suffix = suffix + jnp.where(sub2 < S - sh, pltpu.roll(suffix, S - sh, 0), 0.0)
        density_grad = STEP * (wg * expi[d] - (suffix - own) - behind[d : d + 1, :])
        lg = lgs[d]
        sig = 1.0 / (1.0 + jnp.exp(-lg))
        lgrad[d] = (density_grad * sig).astype(BF16).astype(F32)

    def wait_e(e, c):
        e_copy(e, (m + e) % CHIPS).wait_recv()
        return c

    lax.fori_loop(1, CHIPS, wait_e, 0)
    err_sum = elat[0]
    for k in range(1, CHIPS):
        err_sum = err_sum + elat[k]
    epsend[...] = err_sum
    ep_copy = rc(epsend, eprec, s_ep, r_ep, me, sib)
    ep_copy.start()

    g1_ref[...] = jnp.zeros_like(g1_ref)
    g2_ref[...] = jnp.zeros_like(g2_ref)

    def masked_back_two(d, out):
        lg = lgrad[d]
        lg8 = jnp.concatenate(
            [jnp.broadcast_to(lg[s : s + 1, :], (8, R)) for s in range(S)], axis=1
        )
        for s in range(S):
            cols = slice(s * R, (s + 1) * R)
            v = b2p[d, :, cols] + wdb[...] * lg[s : s + 1, :]
            out[:, cols] = jnp.where(
                h2s[d, :, cols] > 0, v.astype(BF16), jnp.zeros_like(v, BF16)
            )
        return mm(lg8.astype(BF16), h2s[d], NT)

    def masked_back_one(d, b2):
        b1 = mm(w2_ref[...], b2[...], NN).astype(BF16)
        return jnp.where(h1s[d] > 0, b1, jnp.zeros_like(b1))

    def last_step(i, gdens):
        d, e = 2 * i, 2 * i + 1
        gdens = gdens + masked_back_two(d, b2s) + masked_back_two(e, b2t)
        b1s = masked_back_one(d, b2s)
        b1t = masked_back_one(e, b2t)
        g2_ref[...] += mm(h1s[d], b2s[...], NT) + mm(h1s[e], b2t[...], NT)
        g1_ref[...] += mm(take_x(d), b1s, NT) + mm(take_x(e), b1t, NT)
        return gdens

    gdens = lax.fori_loop(0, K // 2, last_step, jnp.zeros((8, HID), F32))
    gd_ref[...] = gdens[0:1]

    ep_copy.wait_recv()
    err_ref[...] = (epsend[0:1, 0:1] + eprec[0:1, 0:1]) * (1.0 / COUNT)

    def end_depth(off, c):
        d = depth_peer(off)
        ds_copy(off, me).wait_send()
        z_copy(d, me).wait_send()
        g_copy(off, me).wait_send()
        d_copy(off, me).wait_send()
        t_copy(off, me).wait_send()
        l_copy(off, g).wait_send()
        b_copy(off, g).wait_send()
        return c

    lax.fori_loop(1, K, end_depth, 0)

    def end_lateral(e, c):
        e_copy(e, m).wait_send()
        return c

    lax.fori_loop(1, CHIPS, end_lateral, 0)

    def end_pair(d, c):
        pf_copy(d).wait_send()
        y_copy(d).wait_send()
        n_copy(d, st).wait_send()
        pb_copy(d, h).wait_send()
        return c

    lax.fori_loop(0, K, end_pair, 0)
    ep_copy.wait_send()


def put_out(*refs):
    for i in range(6):
        refs[6 + i][...] = refs[i][...]


def body(samples, w_first, w_second, w_third, w_density, decoder, depth_order, ray_slot, target):
    vmem = pl.BlockSpec(memory_space=pltpu.VMEM)
    dma = pltpu.SemaphoreType.DMA
    v = pltpu.VMEM
    results = ((ENC, HID), (HID, HID), (HID, FEAT), (1, HID), (3, 1, FEAT), (1, 1))
    outs = pl.pallas_call(
        kernel,
        name="step",
        out_shape=tuple(pltpu.VMEM(shape, F32) for shape in results),
        in_specs=[pl.BlockSpec(memory_space=pl.ANY)] + [vmem] * 5 + [pl.BlockSpec(memory_space=pltpu.SMEM)] + [vmem] * 2,
        out_specs=(vmem,) * 6,
        scratch_shapes=[
            v((S, ENC, K * R), BF16),
            v((HID, ENC), BF16),
            v((HID, HID), BF16),
            v((FEAT, HID), BF16),
            v((HID, R), F32),
            v((K, HID, W), BF16),
            v((K, HID, W), BF16),
            v((K, FEAT, W), BF16),
            v((K, S, R), F32),
            v((K, S, R), F32),
            v((K, S, R), F32),
            v((K, HALF, 2 * R), F32),
            v((K, R), F32),
            v((K, HALF, 2 * R), BF16),
            v((K, 2 * R, 2 * R), BF16),
            v((K, 2, 2, R // 2, HALF), BF16),
            v((K, 2, R // 2, HALF), BF16),
            v((K, R // 2, HALF), BF16),
            v((K, R // 2, HALF), BF16),
            v((K, R // 2, HALF), BF16),
            v((K, R // 2, HALF), BF16),
            v((G, 8, HALF), F32),
            v((G, 8, HALF), F32),
            v((G, 8, HALF), F32),
            v((G, 8, HALF), F32),
            v((K, 2, 2, R // 2, HALF), BF16),
            v((K, K, R), F32),
            v((K, K, R), F32),
            v((K, S, R), F32),
            v((K, S, R), F32),
            v((HID, W), BF16),
            v((HID, W), BF16),
            v((K, HID, W), F32),
            v((K, 8, HALF), F32),
            v((8, R), F32),
            v((CHIPS, 8, R), F32),
            v((8, R), F32),
            v((8, R), F32),
            dma((S,)),
            dma((K,)), dma((K,)),
            dma((K,)), dma((K,)),
            dma((K,)), dma((K,)),
            dma((K,)), dma((K,)),
            dma((G,)), dma((G,)),
            dma((G,)), dma((G,)),
            dma((K,)), dma((K,)),
            dma((K,)), dma((K,)),
            dma((K,)), dma((K,)),
            dma((K,)), dma((K,)),
            dma((K,)), dma((K,)),
            dma((CHIPS,)), dma((CHIPS,)),
            dma(()), dma(()),
        ],
        compiler_params=pltpu.CompilerParams(
            collective_id=0, has_side_effects=True, vmem_limit_bytes=58 * 1024 * 1024
        ),
    )(
        samples[0, 0],
        w_first[0, 0],
        w_second[0, 0],
        w_third[0, 0],
        w_density[0],
        jnp.transpose(decoder, (1, 0, 2)),
        depth_order,
        ray_slot,
        jnp.transpose(target, (1, 0, 2)),
    )
    outs = pl.pallas_call(
        put_out,
        name="put_out",
        out_shape=tuple(jax.ShapeDtypeStruct(shape, F32) for shape in results),
        in_specs=[vmem] * 6,
        out_specs=(vmem,) * 6,
    )(*[pltpu.with_memory_space_constraint(o, pltpu.VMEM) for o in outs])
    return (
        outs[0][None, None],
        outs[1][None, None],
        outs[2][None, None],
        outs[3][None],
        jnp.transpose(outs[4], (1, 0, 2)),
        outs[5][0, 0],
    )


def solution(mesh):
    placed = (
        P("depth", "lateral", None, None),
        P("depth", "lateral", None, None),
        P("depth", "lateral", None, None),
        P("depth", "lateral", None, None),
        P("depth", "lateral", None),
        P("lateral", None, None),
        P("lateral", None),
        P("lateral", None),
        P("lateral", None, "depth"),
    )
    return jax.shard_map(
        body,
        mesh=mesh,
        in_specs=placed,
        out_specs=(
            P("depth", "lateral", None, None),
            P("depth", "lateral", None, None),
            P("depth", "lateral", None, None),
            P("depth", "lateral", None),
            P("lateral", None, None),
            P(),
        ),
        check_vma=False,
    )
```

```python
import jax
import jax.numpy as jnp
from jax import lax
from jax.experimental import pallas as pl
from jax.experimental.pallas import tpu as pltpu
from jax.sharding import PartitionSpec as P

MESH = pl.DeviceIdType.MESH
F32 = jnp.float32
BF16 = jnp.bfloat16

ENC, HID, FEAT = 64, 256, 512
S = 8
K = 8
R = 128
CHIPS = 16
G = 8
W = S * R
HALF = FEAT // 2
STEP = 0.04
FLOOR = 1e-05
COUNT = 24576.0
NEAR_LAG = 4
PAIR_LAG = 7
FIRST = 3

NN = (((1,), (0,)), ((), ()))
NT = (((1,), (1,)), ((), ()))
TN = (((0,), (0,)), ((), ()))


def mm(a, b, dims):
    return lax.dot_general(a, b, dims, preferred_element_type=F32)


def offset_of(i):
    return 4 + ((i + 1) // 2) * (1 - 2 * (i % 2))


def near_offset_of(i):
    return ((i + 1) // 2) * (2 * (i % 2) - 1) + 8


def kernel(
    x_ref, w1_ref, w2_ref, w3_ref, wd_ref, dec_ref, order_ref, slot_ref, tgt_ref,
    g1_ref, g2_ref, g3_ref, gd_ref, gdec_ref, err_ref,
    xs, w1t, w2t, w3t, wdb, h1s, h2s, feats, lgs, wts, expi, bld, scl, scaled, oh,
    pfull, prec, ysend, yrec, zsend, zrecv, lt, lr, lb, br, gbuf, dsall, tmall, wgs, lgrad, b2s, b2t, b2p,
    decall, esend, elat, epsend, eprec,
    s_x, s_ds, r_ds, s_pf, r_pf, s_y, r_y, s_z, r_z, s_l, r_l, s_b, r_b, s_g, r_g, s_n, r_n, s_pb, r_pb,
    s_t, r_t, s_d, r_d, s_e, r_e, s_ep, r_ep,
):
    me = lax.axis_index("depth")
    lat = lax.axis_index("lateral")
    h = lat % 2
    m = lat // 2
    sib = lat + 1 - 2 * h
    g = m // 2
    st = ((m % 4 + 1) // 2) % 2
    near = (m + 1 - 2 * (m % 2)) * 2 + h

    def chip_of(s, i):
        return (i // 2) * 4 + 2 * (i % 2) + (s + i) % 2

    def depth_peer(off):
        return (me + off) % K

    def rc(src, dst, ssem, rsem, z, l):
        return pltpu.make_async_remote_copy(
            src_ref=src, dst_ref=dst, send_sem=ssem, recv_sem=rsem,
            device_id=(z, l), device_id_type=MESH,
        )

    def x_copy(s):
        cols = pl.ds(pl.multiple_of(s * (K * R), K * R), K * R)
        return pltpu.make_async_copy(x_ref.at[:, cols], xs.at[s], s_x.at[s])

    for s in range(S):
        x_copy(s).start()

    def blocks(ref, n, ssem, rsem):
        part = ref.at[pl.ds(0, n)]
        return rc(part, part, ssem, rsem, depth_peer(1), lat)

    barrier = pltpu.get_barrier_semaphore()

    def greet_depth(e, c):
        pl.semaphore_signal(barrier, inc=1, device_id=((me + e) % K, lat), device_id_type=MESH)
        return c

    def greet_lateral(e, c):
        pl.semaphore_signal(
            barrier, inc=1, device_id=(me, ((m + e) % CHIPS) * 2 + h), device_id_type=MESH
        )
        return c

    lax.fori_loop(1, K, greet_depth, 0)
    lax.fori_loop(1, CHIPS, greet_lateral, 0)
    pl.semaphore_signal(barrier, inc=1, device_id=(me, sib), device_id_type=MESH)

    w1t[...] = w1_ref[...].T
    w2t[...] = w2_ref[...].T
    wd8 = jnp.broadcast_to(wd_ref[...], (8, HID))
    wdb[...] = jnp.broadcast_to(wd_ref[...].astype(F32), (R, HID)).T

    def take_x(d):
        return jnp.concatenate(
            [xs[s, :, pl.ds(pl.multiple_of(d * R, R), R)] for s in range(S)], axis=1
        )

    def first_pass(s, c):
        x_copy(s).wait()
        cols = pl.ds(pl.multiple_of(s * R, R), R)
        h1 = jnp.maximum(mm(w1t[...], xs[s], NN).astype(BF16), 0)
        h2 = jnp.maximum(mm(w2t[...], h1, NN).astype(BF16), 0)
        lg = mm(wd8, h2, NN)
        for d in range(K):
            here = slice(d * R, (d + 1) * R)
            h1s[d, :, cols] = h1[:, here]
            h2s[d, :, cols] = h2[:, here]
            lgs[d, pl.ds(s, 1), :] = lg[0:1, here]
        return c

    lax.fori_loop(0, S, first_pass, 0)

    sub = lax.broadcasted_iota(jnp.int32, (K, S, R), 1)
    logits = lgs[...]
    density = jnp.maximum(logits, 0.0) + jnp.log1p(jnp.exp(-jnp.abs(logits)))
    inc = density
    for sh in (1, 2, 4):
        inc = inc + jnp.where(sub >= sh, pltpu.roll(inc, sh, 1), 0.0)
    wts[...] = jnp.exp(-STEP * (inc - density)) * (1.0 - jnp.exp(-STEP * density))
    expi[...] = jnp.exp(-STEP * inc)
    dsall[me] = STEP * jnp.concatenate([inc[d, S - 1 : S, :] for d in range(K)], axis=0)

    pl.semaphore_wait(barrier, K - 1 + CHIPS - 1 + 1)

    def ds_copy(off, k):
        return rc(dsall.at[k], dsall.at[k], s_ds, r_ds, depth_peer(off), lat)

    def send_ds(off, c):
        ds_copy(off, me).start()
        return c

    lax.fori_loop(1, K, send_ds, 0)
    w3t[...] = w3_ref[...].T

    row = lax.broadcasted_iota(jnp.int32, (2 * R, R), 0)
    code = (chip_of((row // 64) % 2, (row // 8) % G) * 2 + row // R) * 4 + row % 4
    code_lo = jnp.where((row // 4) % 2 == 0, code, -1)
    code_hi = jnp.where((row // 4) % 2 == 1, code, -1)

    def one_hot(d, c):
        slots = slot_ref[:, pl.ds(pl.multiple_of(d * R, R), R)]
        oh[d] = jnp.concatenate(
            [
                jnp.where(code_lo == slots, 1.0, 0.0).astype(BF16),
                jnp.where(code_hi == slots, 1.0, 0.0).astype(BF16),
            ],
            axis=1,
        )
        return c

    lax.fori_loop(0, K, one_hot, 0)

    def second_pass(d, c):
        feats[d] = mm(w3t[...], h2s[d], NN).astype(BF16)
        for f0 in range(0, FEAT, 64):
            total = jnp.zeros((64, R), F32)
            for s in range(S):
                total = total + feats[d, f0 : f0 + 64, s * R : (s + 1) * R].astype(F32) * wts[
                    d, s : s + 1, :
                ]
            fh = f0 // HALF
            bld[d, f0 - fh * HALF : f0 - fh * HALF + 64, fh * R : (fh + 1) * R] = total
        return c

    lax.fori_loop(0, K, second_pass, 0)

    places = []
    mine = jnp.int32(0)
    for k in range(K):
        place = jnp.int32(0)
        for p in range(K):
            place = place + jnp.where(order_ref[0, p] == k, p, 0)
        places.append(place)
    for p in range(K):
        mine = mine + jnp.where(order_ref[0, p] == me, p, 0)

    blocks(dsall, K - 1, s_ds, r_ds).wait_recv()
    before = jnp.zeros((K, R), F32)
    for k in range(K):
        before = before + dsall[k] * jnp.where(places[k] < mine, 1.0, 0.0)
    scl[...] = jnp.exp(-before)

    def pf_copy(d):
        return rc(pfull.at[d, 1 - h], prec.at[d], s_pf, r_pf.at[d], me, sib)

    def y_copy(d):
        return rc(ysend.at[d], yrec.at[d], s_y, r_y.at[d], me, near)

    def z_copy(d, k):
        return rc(zsend.at[d], zrecv.at[k], s_z, r_z, d, lat)

    def make_scaled(i, c):
        d = depth_peer(offset_of(i))
        sc = scl[pl.ds(d, 1), :]
        sc = jnp.concatenate([sc, sc], axis=1)
        scaled[d] = (bld[d] * sc).astype(BF16)
        placed = mm(oh[d], scaled[d], NT).astype(BF16)
        for half in range(2):
            for s in range(2):
                r0 = half * R + s * 64
                pfull[d, half, s] = placed[r0 : r0 + 64]
        pf_copy(d).start()
        return c

    lax.fori_loop(0, K, make_scaled, 0)

    def pair_sum(d, s):
        return pfull[d, h, s].astype(F32) + prec[d, s].astype(F32)

    def send_near(i, c):
        d = depth_peer(offset_of(i))
        pf_copy(d).wait_recv()
        ysend[d] = pair_sum(d, 1 - st).astype(BF16)
        y_copy(d).start()
        return c

    lax.fori_loop(0, K, send_near, 0)

    def group_sum(d):
        y_copy(d).wait_recv()
        return (pair_sum(d, st) + yrec[d].astype(F32)).astype(BF16)

    def send_share(i, c):
        d = depth_peer(offset_of(i))
        zsend[d] = group_sum(d)
        z_copy(d, me).start()
        return c

    lax.fori_loop(0, K - 1, send_share, 0)
    zrecv[me] = group_sum(me)

    blocks(zrecv, K - 1, s_z, r_z).wait_recv()
    total = zrecv[0].astype(F32)
    for k in range(1, K):
        total = total + zrecv[k].astype(F32)
    lt[...] = total.reshape(G, 8, HALF)

    def l_copy(e, src):
        to = (g + e) % G
        return rc(lt.at[to], lr.at[src], s_l, r_l, me, chip_of(st, to) * 2 + h)

    def send_l(e, c):
        l_copy(e, g).start()
        return c

    lax.fori_loop(1, G, send_l, 0)
    lr[g] = lt[g]

    shape3 = (8, 8, 32)
    grp = lax.broadcasted_iota(jnp.int32, shape3, 0)
    rowq = lax.broadcasted_iota(jnp.int32, shape3, 1) % 4
    pix = lax.broadcasted_iota(jnp.int32, shape3, 2)
    chosen = pix == rowq * 8 + grp
    low = lax.broadcasted_iota(jnp.int32, (8, HALF), 0) < 4
    targets = []
    decs = []
    for i in range(3):
        t = jnp.where(chosen, jnp.broadcast_to(tgt_ref[i][None], shape3), 0.0)
        targets.append(jnp.sum(t, axis=2, keepdims=True))
        decs.append(
            jnp.where(
                low,
                jnp.broadcast_to(dec_ref[i, :, 0:HALF], (8, HALF)),
                jnp.broadcast_to(dec_ref[i, :, HALF:FEAT], (8, HALF)),
            )[None]
        )

    def both_halves(v):
        v = jnp.broadcast_to(jnp.sum(v, axis=2, keepdims=True), (8, 8, R))
        return v + pltpu.roll(v, 4, 1)

    def wide(v):
        return jnp.concatenate([v, v], axis=2)

    blocks(lr, G - 1, s_l, r_l).wait_recv()
    mean = lr[...] * 0.25
    inverse = wide(lax.rsqrt(both_halves(mean * mean) * (1.0 / FEAT) + FLOOR))
    normed = mean * inverse
    normed_grad = jnp.zeros((8, 8, HALF), F32)
    square = jnp.zeros((8, 8, R), F32)
    dec_rows = []
    for i in range(3):
        residue = both_halves(normed * decs[i]) - targets[i]
        square = square + residue * residue
        res_wide = wide(residue)
        normed_grad = normed_grad + decs[i] * res_wide
        part = jnp.sum(res_wide * normed, axis=0)
        dec_rows.append(jnp.sum(part[0:4], axis=0, keepdims=True))
        dec_rows.append(jnp.sum(part[4:8], axis=0, keepdims=True))
    along = wide(both_halves(normed_grad * normed)) * (1.0 / FEAT)
    pixel_grad = inverse * (normed_grad - normed * along) * 0.25
    lb[...] = pixel_grad.astype(BF16).astype(F32)

    def b_copy(e, src):
        to = (g + e) % G
        return rc(lb.at[to], br.at[src], s_b, r_b, me, chip_of(st, to) * 2 + h)

    def send_b(e, c):
        b_copy(e, g).start()
        return c

    lax.fori_loop(1, G, send_b, 0)
    br[g] = lb[g]

    err_row = jnp.sum(jnp.sum(square, axis=0), axis=0, keepdims=True) * 0.5
    dec_rows.append(jnp.concatenate([err_row, err_row], axis=1))
    dec_rows.append(jnp.zeros((1, HALF), F32))
    decall[me] = jnp.concatenate(dec_rows, axis=0)

    blocks(br, G - 1, s_b, r_b).wait_recv()
    gbuf[me, h, st] = br[...].reshape(R // 2, HALF).astype(BF16)

    def g_copy(off, k):
        ref = gbuf.at[k, h, st]
        return rc(ref, ref, s_g, r_g.at[k], depth_peer(off), lat)

    def n_copy(d, s):
        ref = gbuf.at[d, h, s]
        return rc(ref, ref, s_n, r_n.at[d], me, near)

    def pb_copy(d, half):
        return rc(gbuf.at[d, half], gbuf.at[d, half], s_pb, r_pb.at[d], me, sib)

    def d_copy(off, k):
        return rc(decall.at[k], decall.at[k], s_d, r_d, depth_peer(off), lat)

    def send_g(i, c):
        g_copy(near_offset_of(i) % K, me).start()
        return c

    lax.fori_loop(1, K, send_g, 0)

    def send_d(off, c):
        d_copy(off, me).start()
        return c

    lax.fori_loop(1, K, send_d, 0)

    def take_share(i):
        d = depth_peer(near_offset_of(i))

        @pl.when(i > 0)
        def _():
            g_copy(near_offset_of(i) % K, d).wait_recv()

        n_copy(d, st).start()

    def pass_share(i):
        d = depth_peer(near_offset_of(i))
        n_copy(d, 1 - st).wait_recv()
        pb_copy(d, h).start()

    def back_share(i):
        d = depth_peer(near_offset_of(i))
        pb_copy(d, 1 - h).wait_recv()
        grads = gbuf[d].reshape(2 * R, HALF)
        ray_grad = mm(grads, oh[d], TN)
        terms = jnp.sum(scaled[d].astype(F32) * ray_grad, axis=0, keepdims=True)
        tmall[me, pl.ds(d, 1), :] = terms[:, 0:R] + terms[:, R : 2 * R]
        sc = scl[pl.ds(d, 1), :]
        bld[d] = ray_grad * jnp.concatenate([sc, sc], axis=1)
        weight_grad = [jnp.zeros((8, R), F32) for _ in range(S)]
        for f0 in range(0, FEAT, 64):
            fh = f0 // HALF
            fg = bld[d, f0 - fh * HALF : f0 - fh * HALF + 64, fh * R : (fh + 1) * R]
            for s in range(S):
                part = feats[d, f0 : f0 + 64, s * R : (s + 1) * R].astype(F32) * fg
                weight_grad[s] = weight_grad[s] + jnp.sum(part.reshape(8, 8, R), axis=0)
                feats[d, f0 : f0 + 64, s * R : (s + 1) * R] = (
                    fg * wts[d, s : s + 1, :]
                ).astype(BF16)
        wgs[d] = jnp.concatenate(
            [jnp.sum(weight_grad[s], axis=0, keepdims=True) for s in range(S)], axis=0
        )

    def third_share(d):
        g3_ref[...] += mm(h2s[d], feats[d], NT)
        b2p[d] = mm(w3_ref[...], feats[d], NN)

    g3_ref[...] = jnp.zeros_like(g3_ref)

    def back_step(i, c):
        @pl.when((i == FIRST) | (i > PAIR_LAG))
        def _():
            back_share(jnp.where(i == FIRST, 0, i - PAIR_LAG))

        @pl.when(i == FIRST + 1)
        def _():
            third_share(me)

        @pl.when(i < K)
        def _():
            take_share(i)

        @pl.when((i == 0) | ((i > NEAR_LAG) & (i < K + NEAR_LAG)))
        def _():
            pass_share(jnp.where(i == 0, 0, i - NEAR_LAG))

        return c

    lax.fori_loop(0, K + PAIR_LAG, back_step, 0)

    def t_copy(off, k):
        return rc(tmall.at[k], tmall.at[k], s_t, r_t, depth_peer(off), lat)

    def send_t(off, c):
        t_copy(off, me).start()
        return c

    lax.fori_loop(1, K, send_t, 0)

    blocks(decall, K - 1, s_d, r_d).wait_recv()
    dec_sum = decall[0]
    for k in range(1, K):
        dec_sum = dec_sum + decall[k]
    for i in range(3):
        gdec_ref[i, :, 0:HALF] = dec_sum[2 * i : 2 * i + 1]
        gdec_ref[i, :, HALF:FEAT] = dec_sum[2 * i + 1 : 2 * i + 2]
    esend[...] = jnp.broadcast_to(dec_sum[6:7, 0:R], (8, R))
    elat[m] = esend[...]

    def e_copy(e, src):
        to = (m + e) % CHIPS
        return rc(esend, elat.at[src], s_e, r_e, me, to * 2 + h)

    def send_e(e, c):
        e_copy(e, m).start()
        return c

    lax.fori_loop(1, CHIPS, send_e, 0)

    def third_step(i, c):
        third_share(depth_peer(i))
        return c

    lax.fori_loop(1, K, third_step, 0)

    blocks(tmall, K - 1, s_t, r_t).wait_recv()
    behind = jnp.zeros((K, R), F32)
    for k in range(K):
        behind = behind + tmall[k] * jnp.where(places[k] > mine, 1.0, 0.0)
    sub2 = lax.broadcasted_iota(jnp.int32, (S, R), 0)
    for d in range(K):
        wg = wgs[d]
        own = wg * wts[d]
        suffix = own
        for sh in (1, 2, 4):
            suffix = suffix + jnp.where(sub2 < S - sh, pltpu.roll(suffix, S - sh, 0), 0.0)
        density_grad = STEP * (wg * expi[d] - (suffix - own) - behind[d : d + 1, :])
        lg = lgs[d]
        sig = 1.0 / (1.0 + jnp.exp(-lg))
        lgrad[d] = (density_grad * sig).astype(BF16).astype(F32)

    blocks(elat, CHIPS - 1, s_e, r_e).wait_recv()
    err_sum = elat[0]
    for k in range(1, CHIPS):
        err_sum = err_sum + elat[k]
    epsend[...] = err_sum
    ep_copy = rc(epsend, eprec, s_ep, r_ep, me, sib)
    ep_copy.start()

    g1_ref[...] = jnp.zeros_like(g1_ref)
    g2_ref[...] = jnp.zeros_like(g2_ref)

    def masked_back_two(d, out):
        lg = lgrad[d]
        lg8 = jnp.concatenate(
            [jnp.broadcast_to(lg[s : s + 1, :], (8, R)) for s in range(S)], axis=1
        )
        for s in range(S):
            cols = slice(s * R, (s + 1) * R)
            v = b2p[d, :, cols] + wdb[...] * lg[s : s + 1, :]
            out[:, cols] = jnp.where(
                h2s[d, :, cols] > 0, v.astype(BF16), jnp.zeros_like(v, BF16)
            )
        return mm(lg8.astype(BF16), h2s[d], NT)

    def masked_back_one(d, b2):
        b1 = mm(w2_ref[...], b2[...], NN).astype(BF16)
        return jnp.where(h1s[d] > 0, b1, jnp.zeros_like(b1))

    def last_step(i, gdens):
        d, e = 2 * i, 2 * i + 1
        gdens = gdens + masked_back_two(d, b2s) + masked_back_two(e, b2t)
        b1s = masked_back_one(d, b2s)
        b1t = masked_back_one(e, b2t)
        g2_ref[...] += mm(h1s[d], b2s[...], NT) + mm(h1s[e], b2t[...], NT)
        g1_ref[...] += mm(take_x(d), b1s, NT) + mm(take_x(e), b1t, NT)
        return gdens

    gdens = lax.fori_loop(0, K // 2, last_step, jnp.zeros((8, HID), F32))
    gd_ref[...] = gdens[0:1]

    ep_copy.wait_recv()
    err_ref[...] = (epsend[0:1, 0:1] + eprec[0:1, 0:1]) * (1.0 / COUNT)

    blocks(dsall, K - 1, s_ds, r_ds).wait_send()
    blocks(prec, K, s_pf, r_pf.at[0]).wait_send()
    blocks(ysend, K, s_y, r_y.at[0]).wait_send()
    blocks(zsend, K - 1, s_z, r_z).wait_send()
    blocks(lt, G - 1, s_l, r_l).wait_send()
    blocks(lb, G - 1, s_b, r_b).wait_send()
    blocks(zsend, K - 1, s_g, r_g.at[0]).wait_send()
    blocks(ysend, K, s_n, r_n.at[0]).wait_send()
    blocks(prec, K, s_pb, r_pb.at[0]).wait_send()
    blocks(decall, K - 1, s_d, r_d).wait_send()
    blocks(tmall, K - 1, s_t, r_t).wait_send()
    blocks(elat, CHIPS - 1, s_e, r_e).wait_send()
    ep_copy.wait_send()


def put_out(*refs):
    for i in range(6):
        refs[6 + i][...] = refs[i][...]


def body(samples, w_first, w_second, w_third, w_density, decoder, depth_order, ray_slot, target):
    vmem = pl.BlockSpec(memory_space=pltpu.VMEM)
    dma = pltpu.SemaphoreType.DMA
    v = pltpu.VMEM
    results = ((ENC, HID), (HID, HID), (HID, FEAT), (1, HID), (3, 1, FEAT), (1, 1))
    outs = pl.pallas_call(
        kernel,
        name="step",
        out_shape=tuple(pltpu.VMEM(shape, F32) for shape in results),
        in_specs=[pl.BlockSpec(memory_space=pl.ANY)] + [vmem] * 5 + [pl.BlockSpec(memory_space=pltpu.SMEM)] + [vmem] * 2,
        out_specs=(vmem,) * 6,
        scratch_shapes=[
            v((S, ENC, K * R), BF16),
            v((HID, ENC), BF16),
            v((HID, HID), BF16),
            v((FEAT, HID), BF16),
            v((HID, R), F32),
            v((K, HID, W), BF16),
            v((K, HID, W), BF16),
            v((K, FEAT, W), BF16),
            v((K, S, R), F32),
            v((K, S, R), F32),
            v((K, S, R), F32),
            v((K, HALF, 2 * R), F32),
            v((K, R), F32),
            v((K, HALF, 2 * R), BF16),
            v((K, 2 * R, 2 * R), BF16),
            v((K, 2, 2, R // 2, HALF), BF16),
            v((K, 2, R // 2, HALF), BF16),
            v((K, R // 2, HALF), BF16),
            v((K, R // 2, HALF), BF16),
            v((K, R // 2, HALF), BF16),
            v((K, R // 2, HALF), BF16),
            v((G, 8, HALF), F32),
            v((G, 8, HALF), F32),
            v((G, 8, HALF), F32),
            v((G, 8, HALF), F32),
            v((K, 2, 2, R // 2, HALF), BF16),
            v((K, K, R), F32),
            v((K, K, R), F32),
            v((K, S, R), F32),
            v((K, S, R), F32),
            v((HID, W), BF16),
            v((HID, W), BF16),
            v((K, HID, W), F32),
            v((K, 8, HALF), F32),
            v((8, R), F32),
            v((CHIPS, 8, R), F32),
            v((8, R), F32),
            v((8, R), F32),
            dma((S,)),
            dma(()), dma(()),
            dma(()), dma((K,)),
            dma(()), dma((K,)),
            dma(()), dma(()),
            dma(()), dma(()),
            dma(()), dma(()),
            dma(()), dma((K,)),
            dma(()), dma((K,)),
            dma(()), dma((K,)),
            dma(()), dma(()),
            dma(()), dma(()),
            dma(()), dma(()),
            dma(()), dma(()),
        ],
        compiler_params=pltpu.CompilerParams(
            collective_id=0, has_side_effects=True, vmem_limit_bytes=58 * 1024 * 1024
        ),
    )(
        samples[0, 0],
        w_first[0, 0],
        w_second[0, 0],
        w_third[0, 0],
        w_density[0],
        jnp.transpose(decoder, (1, 0, 2)),
        depth_order,
        ray_slot,
        jnp.transpose(target, (1, 0, 2)),
    )
    outs = pl.pallas_call(
        put_out,
        name="put_out",
        out_shape=tuple(jax.ShapeDtypeStruct(shape, F32) for shape in results),
        in_specs=[vmem] * 6,
        out_specs=(vmem,) * 6,
    )(*[pltpu.with_memory_space_constraint(o, pltpu.VMEM) for o in outs])
    return (
        outs[0][None, None],
        outs[1][None, None],
        outs[2][None, None],
        outs[3][None],
        jnp.transpose(outs[4], (1, 0, 2)),
        outs[5][0, 0],
    )


def solution(mesh):
    placed = (
        P("depth", "lateral", None, None),
        P("depth", "lateral", None, None),
        P("depth", "lateral", None, None),
        P("depth", "lateral", None, None),
        P("depth", "lateral", None),
        P("lateral", None, None),
        P("lateral", None),
        P("lateral", None),
        P("lateral", None, "depth"),
    )
    return jax.shard_map(
        body,
        mesh=mesh,
        in_specs=placed,
        out_specs=(
            P("depth", "lateral", None, None),
            P("depth", "lateral", None, None),
            P("depth", "lateral", None, None),
            P("depth", "lateral", None),
            P("lateral", None, None),
            P(),
        ),
        check_vma=False,
    )
```

```python
import jax
import jax.numpy as jnp
from jax import lax
from jax.experimental import pallas as pl
from jax.experimental.pallas import tpu as pltpu
from jax.sharding import PartitionSpec as P

MESH = pl.DeviceIdType.MESH
F32 = jnp.float32
BF16 = jnp.bfloat16

ENC, HID, FEAT = 64, 256, 512
S = 8
K = 8
R = 128
CHIPS = 16
G = 8
W = S * R
HALF = FEAT // 2
STEP = 0.04
FLOOR = 1e-05
COUNT = 24576.0
NEAR_LAG = 4
PAIR_LAG = 7
FIRST = 3

NN = (((1,), (0,)), ((), ()))
NT = (((1,), (1,)), ((), ()))
TN = (((0,), (0,)), ((), ()))


def mm(a, b, dims):
    return lax.dot_general(a, b, dims, preferred_element_type=F32)


def offset_of(i):
    return 4 + ((i + 1) // 2) * (1 - 2 * (i % 2))


def near_offset_of(i):
    return ((i + 1) // 2) * (2 * (i % 2) - 1) + 8


def kernel(
    x_ref, w1_ref, w2_ref, w3_hbm, wd_ref, dec_ref, order_ref, slot_ref, tgt_ref,
    g1_ref, g2_ref, g3_ref, gd_ref, gdec_ref, err_ref,
    w3_ref, xs, w1t, w2t, w3t, wdb, h1s, h2s, feats, lgs, wts, expi, bld, scl, scaled, oh,
    pfull, prec, ysend, yrec, zsend, zrecv, lt, lr, lb, br, gbuf, dsall, tmall, wgs, lgrad, b2s, b2t, b2p,
    decall, esend, elat, epsend, eprec,
    s_w, s_x, s_ds, r_ds, s_pf, r_pf, s_y, r_y, s_z, r_z, s_l, r_l, s_b, r_b, s_g, r_g, s_n, r_n, s_pb, r_pb,
    s_t, r_t, s_d, r_d, s_e, r_e, s_ep, r_ep,
):
    me = lax.axis_index("depth")
    lat = lax.axis_index("lateral")
    h = lat % 2
    m = lat // 2
    sib = lat + 1 - 2 * h
    g = m // 2
    st = ((m % 4 + 1) // 2) % 2
    near = (m + 1 - 2 * (m % 2)) * 2 + h

    def chip_of(s, i):
        return (i // 2) * 4 + 2 * (i % 2) + (s + i) % 2

    def depth_peer(off):
        return (me + off) % K

    def rc(src, dst, ssem, rsem, z, l):
        return pltpu.make_async_remote_copy(
            src_ref=src, dst_ref=dst, send_sem=ssem, recv_sem=rsem,
            device_id=(z, l), device_id_type=MESH,
        )

    def x_copy(s):
        cols = pl.ds(pl.multiple_of(s * (K * R), K * R), K * R)
        return pltpu.make_async_copy(x_ref.at[:, cols], xs.at[s], s_x.at[s])

    for s in range(S):
        x_copy(s).start()
    w3_copy = pltpu.make_async_copy(w3_hbm, w3_ref, s_w)
    w3_copy.start()

    def blocks(ref, n, ssem, rsem):
        part = ref.at[pl.ds(0, n)]
        return rc(part, part, ssem, rsem, depth_peer(1), lat)

    barrier = pltpu.get_barrier_semaphore()

    def greet_depth(e, c):
        pl.semaphore_signal(barrier, inc=1, device_id=((me + e) % K, lat), device_id_type=MESH)
        return c

    def greet_lateral(e, c):
        pl.semaphore_signal(
            barrier, inc=1, device_id=(me, ((m + e) % CHIPS) * 2 + h), device_id_type=MESH
        )
        return c

    lax.fori_loop(1, K, greet_depth, 0)
    lax.fori_loop(1, CHIPS, greet_lateral, 0)
    pl.semaphore_signal(barrier, inc=1, device_id=(me, sib), device_id_type=MESH)

    w1t[...] = w1_ref[...].T
    w2t[...] = w2_ref[...].T
    wd8 = jnp.broadcast_to(wd_ref[...], (8, HID))

    def take_x(d):
        return jnp.concatenate(
            [xs[s, :, pl.ds(pl.multiple_of(d * R, R), R)] for s in range(S)], axis=1
        )

    def first_pass(s, c):
        x_copy(s).wait()
        cols = pl.ds(pl.multiple_of(s * R, R), R)
        h1 = jnp.maximum(mm(w1t[...], xs[s], NN).astype(BF16), 0)
        h2 = jnp.maximum(mm(w2t[...], h1, NN).astype(BF16), 0)
        lg = mm(wd8, h2, NN)
        for d in range(K):
            here = slice(d * R, (d + 1) * R)
            h1s[d, :, cols] = h1[:, here]
            h2s[d, :, cols] = h2[:, here]
            lgs[d, pl.ds(s, 1), :] = lg[0:1, here]
        return c

    lax.fori_loop(0, S, first_pass, 0)

    sub = lax.broadcasted_iota(jnp.int32, (K, S, R), 1)
    logits = lgs[...]
    density = jnp.maximum(logits, 0.0) + jnp.log1p(jnp.exp(-jnp.abs(logits)))
    inc = density
    for sh in (1, 2, 4):
        inc = inc + jnp.where(sub >= sh, pltpu.roll(inc, sh, 1), 0.0)
    dsall[me] = STEP * jnp.concatenate([inc[d, S - 1 : S, :] for d in range(K)], axis=0)

    pl.semaphore_wait(barrier, K - 1 + CHIPS - 1 + 1)

    def ds_copy(off, k):
        return rc(dsall.at[k], dsall.at[k], s_ds, r_ds, depth_peer(off), lat)

    def send_ds(off, c):
        ds_copy(off, me).start()
        return c

    lax.fori_loop(1, K, send_ds, 0)
    w3_copy.wait()
    w3t[...] = w3_ref[...].T
    wdb[...] = jnp.broadcast_to(wd_ref[...].astype(F32), (R, HID)).T
    wts[...] = jnp.exp(-STEP * (inc - density)) * (1.0 - jnp.exp(-STEP * density))
    expi[...] = jnp.exp(-STEP * inc)

    row = lax.broadcasted_iota(jnp.int32, (2 * R, R), 0)
    code = (chip_of((row // 64) % 2, (row // 8) % G) * 2 + row // R) * 4 + row % 4
    code_lo = jnp.where((row // 4) % 2 == 0, code, -1)
    code_hi = jnp.where((row // 4) % 2 == 1, code, -1)

    def one_hot(d, c):
        slots = slot_ref[:, pl.ds(pl.multiple_of(d * R, R), R)]
        oh[d] = jnp.concatenate(
            [
                jnp.where(code_lo == slots, 1.0, 0.0).astype(BF16),
                jnp.where(code_hi == slots, 1.0, 0.0).astype(BF16),
            ],
            axis=1,
        )
        return c

    lax.fori_loop(0, K, one_hot, 0)

    def second_pass(d, c):
        feats[d] = mm(w3t[...], h2s[d], NN).astype(BF16)
        for f0 in range(0, FEAT, 64):
            total = jnp.zeros((64, R), F32)
            for s in range(S):
                total = total + feats[d, f0 : f0 + 64, s * R : (s + 1) * R].astype(F32) * wts[
                    d, s : s + 1, :
                ]
            fh = f0 // HALF
            bld[d, f0 - fh * HALF : f0 - fh * HALF + 64, fh * R : (fh + 1) * R] = total
        return c

    lax.fori_loop(0, K, second_pass, 0)

    places = []
    mine = jnp.int32(0)
    for k in range(K):
        place = jnp.int32(0)
        for p in range(K):
            place = place + jnp.where(order_ref[0, p] == k, p, 0)
        places.append(place)
    for p in range(K):
        mine = mine + jnp.where(order_ref[0, p] == me, p, 0)

    blocks(dsall, K - 1, s_ds, r_ds).wait_recv()
    before = jnp.zeros((K, R), F32)
    for k in range(K):
        before = before + dsall[k] * jnp.where(places[k] < mine, 1.0, 0.0)
    scl[...] = jnp.exp(-before)

    def pf_copy(d):
        return rc(pfull.at[d, 1 - h], prec.at[d], s_pf, r_pf.at[d], me, sib)

    def y_copy(d):
        return rc(ysend.at[d], yrec.at[d], s_y, r_y.at[d], me, near)

    def z_copy(d, k):
        return rc(zsend.at[d], zrecv.at[k], s_z, r_z, d, lat)

    def make_scaled(i, c):
        d = depth_peer(offset_of(i))
        sc = scl[pl.ds(d, 1), :]
        sc = jnp.concatenate([sc, sc], axis=1)
        scaled[d] = (bld[d] * sc).astype(BF16)
        placed = mm(oh[d], scaled[d], NT).astype(BF16)
        for half in range(2):
            for s in range(2):
                r0 = half * R + s * 64
                pfull[d, half, s] = placed[r0 : r0 + 64]
        pf_copy(d).start()
        return c

    lax.fori_loop(0, K, make_scaled, 0)

    def pair_sum(d, s):
        return pfull[d, h, s].astype(F32) + prec[d, s].astype(F32)

    def send_near(i, c):
        d = depth_peer(offset_of(i))
        pf_copy(d).wait_recv()
        ysend[d] = pair_sum(d, 1 - st).astype(BF16)
        y_copy(d).start()
        return c

    lax.fori_loop(0, K, send_near, 0)

    def group_sum(d):
        y_copy(d).wait_recv()
        return (pair_sum(d, st) + yrec[d].astype(F32)).astype(BF16)

    def send_share(i, c):
        d = depth_peer(offset_of(i))
        zsend[d] = group_sum(d)
        z_copy(d, me).start()
        return c

    lax.fori_loop(0, K - 1, send_share, 0)
    zrecv[me] = group_sum(me)

    blocks(zrecv, K - 1, s_z, r_z).wait_recv()
    total = zrecv[0].astype(F32)
    for k in range(1, K):
        total = total + zrecv[k].astype(F32)
    lt[...] = total.reshape(G, 8, HALF)

    def l_copy(e, src):
        to = (g + e) % G
        return rc(lt.at[to], lr.at[src], s_l, r_l, me, chip_of(st, to) * 2 + h)

    def send_l(e, c):
        l_copy(e, g).start()
        return c

    lax.fori_loop(1, G, send_l, 0)
    lr[g] = lt[g]

    shape3 = (8, 8, 32)
    grp = lax.broadcasted_iota(jnp.int32, shape3, 0)
    rowq = lax.broadcasted_iota(jnp.int32, shape3, 1) % 4
    pix = lax.broadcasted_iota(jnp.int32, shape3, 2)
    chosen = pix == rowq * 8 + grp
    low = lax.broadcasted_iota(jnp.int32, (8, HALF), 0) < 4
    targets = []
    decs = []
    for i in range(3):
        t = jnp.where(chosen, jnp.broadcast_to(tgt_ref[i][None], shape3), 0.0)
        targets.append(jnp.sum(t, axis=2, keepdims=True))
        decs.append(
            jnp.where(
                low,
                jnp.broadcast_to(dec_ref[i, :, 0:HALF], (8, HALF)),
                jnp.broadcast_to(dec_ref[i, :, HALF:FEAT], (8, HALF)),
            )[None]
        )

    def both_halves(v):
        v = jnp.broadcast_to(jnp.sum(v, axis=2, keepdims=True), (8, 8, R))
        return v + pltpu.roll(v, 4, 1)

    def wide(v):
        return jnp.concatenate([v, v], axis=2)

    blocks(lr, G - 1, s_l, r_l).wait_recv()
    mean = lr[...] * 0.25
    inverse = wide(lax.rsqrt(both_halves(mean * mean) * (1.0 / FEAT) + FLOOR))
    normed = mean * inverse
    normed_grad = jnp.zeros((8, 8, HALF), F32)
    square = jnp.zeros((8, 8, R), F32)
    dec_rows = []
    for i in range(3):
        residue = both_halves(normed * decs[i]) - targets[i]
        square = square + residue * residue
        res_wide = wide(residue)
        normed_grad = normed_grad + decs[i] * res_wide
        part = jnp.sum(res_wide * normed, axis=0)
        dec_rows.append(jnp.sum(part[0:4], axis=0, keepdims=True))
        dec_rows.append(jnp.sum(part[4:8], axis=0, keepdims=True))
    along = wide(both_halves(normed_grad * normed)) * (1.0 / FEAT)
    pixel_grad = inverse * (normed_grad - normed * along) * 0.25
    lb[...] = pixel_grad.astype(BF16).astype(F32)

    def b_copy(e, src):
        to = (g + e) % G
        return rc(lb.at[to], br.at[src], s_b, r_b, me, chip_of(st, to) * 2 + h)

    def send_b(e, c):
        b_copy(e, g).start()
        return c

    lax.fori_loop(1, G, send_b, 0)
    br[g] = lb[g]

    err_row = jnp.sum(jnp.sum(square, axis=0), axis=0, keepdims=True) * 0.5
    dec_rows.append(jnp.concatenate([err_row, err_row], axis=1))
    dec_rows.append(jnp.zeros((1, HALF), F32))
    decall[me] = jnp.concatenate(dec_rows, axis=0)

    blocks(br, G - 1, s_b, r_b).wait_recv()
    gbuf[me, h, st] = br[...].reshape(R // 2, HALF).astype(BF16)

    def g_copy(off, k):
        ref = gbuf.at[k, h, st]
        return rc(ref, ref, s_g, r_g.at[k], depth_peer(off), lat)

    def n_copy(d, s):
        ref = gbuf.at[d, h, s]
        return rc(ref, ref, s_n, r_n.at[d], me, near)

    def pb_copy(d, half):
        return rc(gbuf.at[d, half], gbuf.at[d, half], s_pb, r_pb.at[d], me, sib)

    def d_copy(off, k):
        return rc(decall.at[k], decall.at[k], s_d, r_d, depth_peer(off), lat)

    def send_g(i, c):
        g_copy(near_offset_of(i) % K, me).start()
        return c

    lax.fori_loop(1, K, send_g, 0)

    def send_d(off, c):
        d_copy(off, me).start()
        return c

    lax.fori_loop(1, K, send_d, 0)

    def take_share(i):
        d = depth_peer(near_offset_of(i))

        @pl.when(i > 0)
        def _():
            g_copy(near_offset_of(i) % K, d).wait_recv()

        n_copy(d, st).start()

    def pass_share(i):
        d = depth_peer(near_offset_of(i))
        n_copy(d, 1 - st).wait_recv()
        pb_copy(d, h).start()

    def back_share(i):
        d = depth_peer(near_offset_of(i))
        pb_copy(d, 1 - h).wait_recv()
        grads = gbuf[d].reshape(2 * R, HALF)
        ray_grad = mm(grads, oh[d], TN)
        terms = jnp.sum(scaled[d].astype(F32) * ray_grad, axis=0, keepdims=True)
        tmall[me, pl.ds(d, 1), :] = terms[:, 0:R] + terms[:, R : 2 * R]
        sc = scl[pl.ds(d, 1), :]
        bld[d] = ray_grad * jnp.concatenate([sc, sc], axis=1)
        weight_grad = [jnp.zeros((8, R), F32) for _ in range(S)]
        for f0 in range(0, FEAT, 64):
            fh = f0 // HALF
            fg = bld[d, f0 - fh * HALF : f0 - fh * HALF + 64, fh * R : (fh + 1) * R]
            for s in range(S):
                part = feats[d, f0 : f0 + 64, s * R : (s + 1) * R].astype(F32) * fg
                weight_grad[s] = weight_grad[s] + jnp.sum(part.reshape(8, 8, R), axis=0)
                feats[d, f0 : f0 + 64, s * R : (s + 1) * R] = (
                    fg * wts[d, s : s + 1, :]
                ).astype(BF16)
        wgs[d] = jnp.concatenate(
            [jnp.sum(weight_grad[s], axis=0, keepdims=True) for s in range(S)], axis=0
        )

    def third_share(d):
        g3_ref[...] += mm(h2s[d], feats[d], NT)
        b2p[d] = mm(w3_ref[...], feats[d], NN)

    g3_ref[...] = jnp.zeros_like(g3_ref)

    def back_step(i, c):
        @pl.when((i == FIRST) | (i > PAIR_LAG))
        def _():
            back_share(jnp.where(i == FIRST, 0, i - PAIR_LAG))

        @pl.when(i == FIRST + 1)
        def _():
            third_share(me)

        @pl.when(i < K)
        def _():
            take_share(i)

        @pl.when((i == 0) | ((i > NEAR_LAG) & (i < K + NEAR_LAG)))
        def _():
            pass_share(jnp.where(i == 0, 0, i - NEAR_LAG))

        return c

    lax.fori_loop(0, K + PAIR_LAG, back_step, 0)

    def t_copy(off, k):
        return rc(tmall.at[k], tmall.at[k], s_t, r_t, depth_peer(off), lat)

    def send_t(off, c):
        t_copy(off, me).start()
        return c

    lax.fori_loop(1, K, send_t, 0)

    blocks(decall, K - 1, s_d, r_d).wait_recv()
    dec_sum = decall[0]
    for k in range(1, K):
        dec_sum = dec_sum + decall[k]
    for i in range(3):
        gdec_ref[i, :, 0:HALF] = dec_sum[2 * i : 2 * i + 1]
        gdec_ref[i, :, HALF:FEAT] = dec_sum[2 * i + 1 : 2 * i + 2]
    esend[...] = jnp.broadcast_to(dec_sum[6:7, 0:R], (8, R))
    elat[m] = esend[...]

    def e_copy(e, src):
        to = (m + e) % CHIPS
        return rc(esend, elat.at[src], s_e, r_e, me, to * 2 + h)

    def send_e(e, c):
        e_copy(e, m).start()
        return c

    lax.fori_loop(1, CHIPS, send_e, 0)

    def third_step(i, c):
        third_share(depth_peer(i))
        return c

    lax.fori_loop(1, K, third_step, 0)

    blocks(tmall, K - 1, s_t, r_t).wait_recv()
    behind = jnp.zeros((K, R), F32)
    for k in range(K):
        behind = behind + tmall[k] * jnp.where(places[k] > mine, 1.0, 0.0)
    sub2 = lax.broadcasted_iota(jnp.int32, (S, R), 0)
    for d in range(K):
        wg = wgs[d]
        own = wg * wts[d]
        suffix = own
        for sh in (1, 2, 4):
            suffix = suffix + jnp.where(sub2 < S - sh, pltpu.roll(suffix, S - sh, 0), 0.0)
        density_grad = STEP * (wg * expi[d] - (suffix - own) - behind[d : d + 1, :])
        lg = lgs[d]
        sig = 1.0 / (1.0 + jnp.exp(-lg))
        lgrad[d] = (density_grad * sig).astype(BF16).astype(F32)

    blocks(elat, CHIPS - 1, s_e, r_e).wait_recv()
    err_sum = elat[0]
    for k in range(1, CHIPS):
        err_sum = err_sum + elat[k]
    epsend[...] = err_sum
    ep_copy = rc(epsend, eprec, s_ep, r_ep, me, sib)
    ep_copy.start()

    g1_ref[...] = jnp.zeros_like(g1_ref)
    g2_ref[...] = jnp.zeros_like(g2_ref)

    def masked_back_two(d, out):
        lg = lgrad[d]
        lg8 = jnp.concatenate(
            [jnp.broadcast_to(lg[s : s + 1, :], (8, R)) for s in range(S)], axis=1
        )
        for s in range(S):
            cols = slice(s * R, (s + 1) * R)
            v = b2p[d, :, cols] + wdb[...] * lg[s : s + 1, :]
            out[:, cols] = jnp.where(
                h2s[d, :, cols] > 0, v.astype(BF16), jnp.zeros_like(v, BF16)
            )
        return mm(lg8.astype(BF16), h2s[d], NT)

    def masked_back_one(d, b2):
        b1 = mm(w2_ref[...], b2[...], NN).astype(BF16)
        return jnp.where(h1s[d] > 0, b1, jnp.zeros_like(b1))

    def last_step(i, gdens):
        d, e = 2 * i, 2 * i + 1
        gdens = gdens + masked_back_two(d, b2s) + masked_back_two(e, b2t)
        b1s = masked_back_one(d, b2s)
        b1t = masked_back_one(e, b2t)
        g2_ref[...] += mm(h1s[d], b2s[...], NT) + mm(h1s[e], b2t[...], NT)
        g1_ref[...] += mm(take_x(d), b1s, NT) + mm(take_x(e), b1t, NT)
        return gdens

    gdens = lax.fori_loop(0, K // 2, last_step, jnp.zeros((8, HID), F32))
    gd_ref[...] = gdens[0:1]

    ep_copy.wait_recv()
    err_ref[...] = (epsend[0:1, 0:1] + eprec[0:1, 0:1]) * (1.0 / COUNT)

    blocks(dsall, K - 1, s_ds, r_ds).wait_send()
    blocks(prec, K, s_pf, r_pf.at[0]).wait_send()
    blocks(ysend, K, s_y, r_y.at[0]).wait_send()
    blocks(zsend, K - 1, s_z, r_z).wait_send()
    blocks(lt, G - 1, s_l, r_l).wait_send()
    blocks(lb, G - 1, s_b, r_b).wait_send()
    blocks(zsend, K - 1, s_g, r_g.at[0]).wait_send()
    blocks(ysend, K, s_n, r_n.at[0]).wait_send()
    blocks(prec, K, s_pb, r_pb.at[0]).wait_send()
    blocks(decall, K - 1, s_d, r_d).wait_send()
    blocks(tmall, K - 1, s_t, r_t).wait_send()
    blocks(elat, CHIPS - 1, s_e, r_e).wait_send()
    ep_copy.wait_send()


def put_out(*refs):
    for i in range(6):
        refs[6 + i][...] = refs[i][...]


def body(samples, w_first, w_second, w_third, w_density, decoder, depth_order, ray_slot, target):
    vmem = pl.BlockSpec(memory_space=pltpu.VMEM)
    hbm = pl.BlockSpec(memory_space=pl.ANY)
    dma = pltpu.SemaphoreType.DMA
    v = pltpu.VMEM
    results = ((ENC, HID), (HID, HID), (HID, FEAT), (1, HID), (3, 1, FEAT), (1, 1))
    outs = pl.pallas_call(
        kernel,
        name="step",
        out_shape=tuple(pltpu.VMEM(shape, F32) for shape in results),
        in_specs=[hbm, vmem, vmem, hbm, vmem, vmem] + [pl.BlockSpec(memory_space=pltpu.SMEM)] + [vmem] * 2,
        out_specs=(vmem,) * 6,
        scratch_shapes=[
            v((HID, FEAT), BF16),
            v((S, ENC, K * R), BF16),
            v((HID, ENC), BF16),
            v((HID, HID), BF16),
            v((FEAT, HID), BF16),
            v((HID, R), F32),
            v((K, HID, W), BF16),
            v((K, HID, W), BF16),
            v((K, FEAT, W), BF16),
            v((K, S, R), F32),
            v((K, S, R), F32),
            v((K, S, R), F32),
            v((K, HALF, 2 * R), F32),
            v((K, R), F32),
            v((K, HALF, 2 * R), BF16),
            v((K, 2 * R, 2 * R), BF16),
            v((K, 2, 2, R // 2, HALF), BF16),
            v((K, 2, R // 2, HALF), BF16),
            v((K, R // 2, HALF), BF16),
            v((K, R // 2, HALF), BF16),
            v((K, R // 2, HALF), BF16),
            v((K, R // 2, HALF), BF16),
            v((G, 8, HALF), F32),
            v((G, 8, HALF), F32),
            v((G, 8, HALF), F32),
            v((G, 8, HALF), F32),
            v((K, 2, 2, R // 2, HALF), BF16),
            v((K, K, R), F32),
            v((K, K, R), F32),
            v((K, S, R), F32),
            v((K, S, R), F32),
            v((HID, W), BF16),
            v((HID, W), BF16),
            v((K, HID, W), F32),
            v((K, 8, HALF), F32),
            v((8, R), F32),
            v((CHIPS, 8, R), F32),
            v((8, R), F32),
            v((8, R), F32),
            dma(()),
            dma((S,)),
            dma(()), dma(()),
            dma(()), dma((K,)),
            dma(()), dma((K,)),
            dma(()), dma(()),
            dma(()), dma(()),
            dma(()), dma(()),
            dma(()), dma((K,)),
            dma(()), dma((K,)),
            dma(()), dma((K,)),
            dma(()), dma(()),
            dma(()), dma(()),
            dma(()), dma(()),
            dma(()), dma(()),
        ],
        compiler_params=pltpu.CompilerParams(
            collective_id=0, has_side_effects=True, vmem_limit_bytes=58 * 1024 * 1024
        ),
    )(
        samples[0, 0],
        w_first[0, 0],
        w_second[0, 0],
        w_third[0, 0],
        w_density[0],
        jnp.transpose(decoder, (1, 0, 2)),
        depth_order,
        ray_slot,
        jnp.transpose(target, (1, 0, 2)),
    )
    outs = pl.pallas_call(
        put_out,
        name="put_out",
        out_shape=tuple(jax.ShapeDtypeStruct(shape, F32) for shape in results),
        in_specs=[vmem] * 6,
        out_specs=(vmem,) * 6,
    )(*[pltpu.with_memory_space_constraint(o, pltpu.VMEM) for o in outs])
    return (
        outs[0][None, None],
        outs[1][None, None],
        outs[2][None, None],
        outs[3][None],
        jnp.transpose(outs[4], (1, 0, 2)),
        outs[5][0, 0],
    )


def solution(mesh):
    placed = (
        P("depth", "lateral", None, None),
        P("depth", "lateral", None, None),
        P("depth", "lateral", None, None),
        P("depth", "lateral", None, None),
        P("depth", "lateral", None),
        P("lateral", None, None),
        P("lateral", None),
        P("lateral", None),
        P("lateral", None, "depth"),
    )
    return jax.shard_map(
        body,
        mesh=mesh,
        in_specs=placed,
        out_specs=(
            P("depth", "lateral", None, None),
            P("depth", "lateral", None, None),
            P("depth", "lateral", None, None),
            P("depth", "lateral", None),
            P("lateral", None, None),
            P(),
        ),
        check_vma=False,
    )
```
